768 devices in a mesh: cell: 32 (over x, y), band: 24 (over z, core).
Axes of the slice: x: 4, y: 8, z: 12, core: 2. Of those that a mesh axis runs over, the one named last changes fastest.
Arguments:
- waves: float32 [1152, 37856], P('band', 'cell'), may hold values from -6 to 6
- cell_matrix: float32 [128, 343, 343], P('cell')
- node_map: int32 [128, 343], P('cell'), may hold values from 0 to 1182, as said below
- share_list: int32 [32, 2, 169], P('cell'), may hold values from 0 to 1182, as said below
- contacts: int32 [2, 512], P(None, 'cell'), may hold values from 0 to 127, as said below
- proj_values: float32 [512, 8, 343], P('cell'), may hold values from -0.3125 to 0.3125
- coupling: float32 [128, 8], replicated, may hold values from -1 to 1
- proj_count: int32 [128], replicated, may hold values from 1 to 8
- mass: float32 [37856], P('cell'), may hold values from 0.5 to 2
Outputs:
- filtered: float32 [1152, 37856], P('band', 'cell')
- gram: float32 [1152, 1152], P('band')
The draws below stay inside these ranges and needn't reach their ends.
Inputs may be any that keep to these rules, and one draw needn't show every extreme that they name: `node_map`: row c holds local node numbers of partition c // 4; the nodes of a cell are distinct and every local node belongs to some cell of its partition. `share_list`: row 0 of partition q lists its local nodes that are also nodes of partition q - 1, row 1 those that are also nodes of partition q + 1, cyclically; the k-th node of row 1 of q is the same node as the k-th node of row 0 of q + 1. Within a partition the two rows are disjoint and their entries distinct. `contacts`: column e belongs to partition e // 16: row 0 is a local cell number below 4, row 1 an atom; no pair of cell and atom repeats within a partition. Each partition is home to 4 atoms, and every entry of an atom lies in its home partition or in one of the two beside it, cyclically.
All inputs are finite; a program needn't handle non-finite values.
Results may differ from the reference program's by a relative error of at most 0.0003.
Values may be sent and summed in bfloat16 or wider, within the bound.
No kernel may reach another device: no remote copies, remote signals or barrier semaphores. Data moves between devices by JAX's collectives and lax.ppermute only.
A program may use at most 32 MiB of HBM per device.

```python
import math
import jax
import jax.numpy as jnp
from jax import lax

BANDS = 1152
DEGREE = 6
CELL_NODES = 343
CHAIN_CELLS = 1
CELLS_DEV = 4
FACE = 169
NODES_DEV = 1183
NODES = 37856
ATOM_DEV = 4
ATOMS = 128
NPROJ = 8
OVL_DEV = 16
OVL = 512
N_CELL = 32


def draw_cell_matrix(key, part):
    key_diag = jax.random.fold_in(key, 3)
    key_noise = jax.random.fold_in(key, 5)
    cell_total = N_CELL * CELLS_DEV
    diagonal_part = jnp.exp(jax.random.uniform(key_diag, (cell_total, CELL_NODES), jnp.float32, math.log(0.05), math.log(0.3)))
    noise_part = jax.random.normal(key_noise, (cell_total, CELL_NODES, CELL_NODES), jnp.float32)
    noise_part = (noise_part + jnp.swapaxes(noise_part, 1, 2)) * (0.01 / math.sqrt(2.0))
    return noise_part + diagonal_part[:, :, None] * jnp.eye(CELL_NODES, dtype=jnp.float32)[None]


def local_numbers(key):
    part_keys = jax.random.split(jax.random.fold_in(key, 11), N_CELL)
    return jax.vmap(lambda one_key: jax.random.permutation(one_key, NODES_DEV))(part_keys).astype(jnp.int32)


def draw_node_map(key, part):
    numbers = local_numbers(key)
    side_nodes = 2 * DEGREE + 1
    edge_nodes = DEGREE + 1
    cell_ids = jnp.arange(CELLS_DEV, dtype=jnp.int32)
    node_ids = jnp.arange(CELL_NODES, dtype=jnp.int32)
    cell_level = cell_ids // 4
    cell_line = cell_ids // 2 % 2
    cell_place = cell_ids % 2
    node_level = node_ids // (edge_nodes * edge_nodes)
    node_line = node_ids // edge_nodes % edge_nodes
    node_place = node_ids % edge_nodes
    canonical = ((cell_level[:, None] * DEGREE + node_level[None, :]) * side_nodes + cell_line[:, None] * DEGREE + node_line[None, :]) * side_nodes + cell_place[:, None] * DEGREE + node_place[None, :]
    return numbers[:, canonical].reshape(N_CELL * CELLS_DEV, CELL_NODES)


def draw_share_list(key, part):
    numbers = local_numbers(key)
    face_ids = jnp.arange(FACE, dtype=jnp.int32)
    top_ids = face_ids + CHAIN_CELLS * DEGREE * FACE
    return jnp.stack([numbers[:, face_ids], numbers[:, top_ids]], axis=1)


def draw_contacts(key, part):
    atom_order = jax.random.permutation(jax.random.fold_in(key, 23), ATOMS).astype(jnp.int32)
    part_keys = jax.random.split(jax.random.fold_in(key, 29), N_CELL)
    pair_total = 3 * ATOM_DEV * CELLS_DEV

    def part_entries(one_key, home_part):
        chosen = jax.random.permutation(one_key, pair_total)[:OVL_DEV].astype(jnp.int32)
        cell_pick = chosen % CELLS_DEV
        remains = chosen // CELLS_DEV
        offset_part = remains // ATOM_DEV - 1
        atom_slot = remains % ATOM_DEV
        atom_home = (home_part + offset_part) % N_CELL
        atom_ids = atom_order[atom_home * ATOM_DEV + atom_slot]
        return jnp.stack([cell_pick, atom_ids])
    entries = jax.vmap(part_entries)(part_keys, jnp.arange(N_CELL, dtype=jnp.int32))
    return entries.transpose(1, 0, 2).reshape(2, N_CELL * OVL_DEV)


def set_ends(values, key, low, top_value):
    spot = [jax.random.randint(jax.random.fold_in(key, axis), (), 0, length) for axis, length in enumerate(values.shape)]
    widest = values.shape.index(max(values.shape))
    beside = spot[:widest] + [(spot[widest] + 1) % values.shape[widest]] + spot[widest + 1:]
    return values.at[tuple(spot)].set(low).at[tuple(beside)].set(top_value)


def block_levels(rng, dims, pieces, least, top_value):
    def one(dim, blocks):
        steps = jax.random.uniform(jax.random.fold_in(jax.random.fold_in(rng, 6), dim), (blocks,), jnp.float32, least / len(pieces), top_value / len(pieces))
        return jnp.repeat(jnp.exp(steps), dims[dim] // blocks).reshape((-1,) + (1,) * (len(dims) - dim - 1))

    factor_of = one(*pieces[0])
    for cut in pieces[1:]:
        factor_of = factor_of * one(*cut)
    return factor_of


def gaussian(rng, shape, width, limit, cuts=(), kind=jnp.bfloat16):
    gain = block_levels(rng, shape, cuts, -0.22, 0.18) if cuts else 1.0
    result = jax.random.normal(rng, shape, jnp.float32) * width * gain
    return jnp.minimum(jnp.maximum(result, -limit), limit).astype(kind)


def setup_inputs(seed: int = 0) -> dict:
    arg_keys = jax.random.split(jax.random.key(seed), 10)
    return {
        "waves": gaussian(arg_keys[0], (BANDS, NODES), 1.0, 6.0, ((0, 24), (1, 32)), jnp.float32),
        "cell_matrix": draw_cell_matrix(jax.random.fold_in(arg_keys[9], 71), 0),
        "node_map": draw_node_map(jax.random.fold_in(arg_keys[9], 71), 0),
        "share_list": draw_share_list(jax.random.fold_in(arg_keys[9], 71), 0),
        "contacts": draw_contacts(jax.random.fold_in(arg_keys[9], 71), 0),
        "proj_values": gaussian(arg_keys[5], (OVL, NPROJ, CELL_NODES), CELL_NODES ** -0.5, 0.3125, ((0, 32),), jnp.float32),
        "coupling": jnp.clip(jax.random.uniform(arg_keys[6], (ATOMS, NPROJ), jnp.float32, -1.0, 1.0), -1.0, 1.0),
        "proj_count": set_ends(jax.random.randint(arg_keys[7], (ATOMS,), 1, NPROJ + 1), jax.random.fold_in(arg_keys[7], 1), 1, NPROJ).astype(jnp.int32),
        "mass": jnp.clip(jnp.exp(math.log(2.0) - 1.3862944 * jax.random.uniform(arg_keys[8], (NODES,), jnp.float32) ** block_levels(arg_keys[8], (NODES,), ((0, 32),), -0.2, 0.2)), 0.5, 2.0),
    }


PRECISE = lax.Precision.HIGHEST
CENTER = 1.0
HALF_WIDTH = 1.0
LOWEST = -0.5

def filter_terms():
    sigma_now = HALF_WIDTH / (LOWEST - CENTER)
    gamma_ratio = 2.0 / sigma_now
    first_scale = sigma_now / HALF_WIDTH
    later_terms = []
    for turn_index in range(2):
        sigma_next = 1.0 / (gamma_ratio - sigma_now)
        later_terms.append((2.0 * sigma_next / HALF_WIDTH, sigma_now * sigma_next))
        sigma_now = sigma_next
    return (first_scale, later_terms)

def atom_partials(values, part_nodes, part_over, part_proj):
    cell_vals = values[:, part_nodes]
    entry_vals = cell_vals[:, part_over[0], :]
    coeffs = jnp.einsum('bei,epi->bep', entry_vals, part_proj, precision=PRECISE)
    onehot_atom = (part_over[1][:, None] == jnp.arange(ATOMS, dtype=jnp.int32)[None, :]).astype(jnp.float32)
    return jnp.einsum('bep,ea->bap', coeffs, onehot_atom, precision=PRECISE)

def assemble_part(values, part_matrix, part_nodes, part_over, part_proj, scaled):
    cell_vals = values[:, part_nodes]
    cell_out = jnp.einsum('bcj,cij->bci', cell_vals, part_matrix, precision=PRECISE)
    onehot_atom = (part_over[1][:, None] == jnp.arange(ATOMS, dtype=jnp.int32)[None, :]).astype(jnp.float32)
    onehot_cell = (part_over[0][:, None] == jnp.arange(CELLS_DEV, dtype=jnp.int32)[None, :]).astype(jnp.float32)
    returned = jnp.einsum('bap,ea->bep', scaled, onehot_atom, precision=PRECISE)
    added_terms = jnp.einsum('bep,epi->bei', returned, part_proj, precision=PRECISE)
    cell_out = cell_out + jnp.einsum('bei,ec->bci', added_terms, onehot_cell, precision=PRECISE)
    return jnp.zeros((BANDS, NODES_DEV), jnp.float32).at[:, part_nodes].add(cell_out)

def take_columns(part_block, node_index):
    return part_block[:, node_index]

def add_faces(part_block, low_index, high_index, low_add, high_add):
    return part_block.at[:, low_index].add(low_add).at[:, high_index].add(high_add)

def reference(waves, cell_matrix, node_map, share_list, contacts, proj_values, coupling, proj_count, mass):
    part_waves = waves.reshape(BANDS, N_CELL, NODES_DEV).transpose(1, 0, 2)
    part_matrix = cell_matrix.reshape(N_CELL, CELLS_DEV, CELL_NODES, CELL_NODES)
    part_nodes = node_map.reshape(N_CELL, CELLS_DEV, CELL_NODES)
    part_over = contacts.reshape(2, N_CELL, OVL_DEV).transpose(1, 0, 2)
    part_proj = proj_values.reshape(N_CELL, OVL_DEV, NPROJ, CELL_NODES)
    part_mass = mass.reshape(N_CELL, NODES_DEV)
    levels = jnp.arange(NPROJ, dtype=jnp.int32)
    scales = coupling * (levels[None, :] < proj_count[:, None]).astype(jnp.float32)

    def apply_operator(values):

        def add_table(running, part_items):
            return (running + atom_partials(part_items[0], part_items[1], part_items[2], part_items[3]), None)
        summed, unused = lax.scan(add_table, jnp.zeros((BANDS, ATOMS, NPROJ), jnp.float32), (values, part_nodes, part_over, part_proj))
        scaled = summed * scales[None]
        assembled = lax.map(lambda part_items: assemble_part(part_items[0], part_items[1], part_items[2], part_items[3], part_items[4], scaled), (values, part_matrix, part_nodes, part_over, part_proj))
        low_faces = jax.vmap(take_columns)(assembled, share_list[:, 0])
        high_faces = jax.vmap(take_columns)(assembled, share_list[:, 1])
        from_prev = jnp.roll(high_faces, 1, axis=0)
        from_next = jnp.roll(low_faces, -1, axis=0)
        return jax.vmap(add_faces)(assembled, share_list[:, 0], share_list[:, 1], from_prev, from_next)
    first_scale, later_terms = filter_terms()
    previous = part_waves
    current = first_scale * (apply_operator(previous) - CENTER * previous)
    for lead_scale, back_scale in later_terms:
        upcoming = lead_scale * (apply_operator(current) - CENTER * current) - back_scale * previous
        previous, current = (current, upcoming)
    owned = jax.vmap(lambda node_index: jnp.ones((NODES_DEV,), jnp.float32).at[node_index].set(0.0))(share_list[:, 0])
    zed = (current * (owned * jnp.sqrt(part_mass))[:, None, :]).astype(jnp.bfloat16)

    def add_gram(running, zed_part):
        return (running + jnp.dot(zed_part, zed_part.T, preferred_element_type=jnp.float32), None)
    summed_gram, unused = lax.scan(add_gram, jnp.zeros((BANDS, BANDS), jnp.float32), zed)
    gram = summed_gram / math.sqrt(N_CELL * NODES_DEV)
    band_ids = jnp.arange(BANDS, dtype=jnp.int32)
    gram = jnp.where(band_ids[:, None] == band_ids[None, :], 0.0, gram)
    filtered = current.transpose(1, 0, 2).reshape(BANDS, N_CELL * NODES_DEV)
    return (filtered, gram)
```

```python
import functools
import math

import jax
import jax.numpy as jnp
from jax import lax
from jax.experimental import pallas as pl
from jax.experimental.pallas import tpu as pltpu
from jax.sharding import PartitionSpec as P

CENTER = 1.0
HALF_WIDTH = 1.0
LOWEST = -0.5
F32 = jnp.float32
BF16 = jnp.bfloat16


def filter_terms():
    sigma_now = HALF_WIDTH / (LOWEST - CENTER)
    gamma_ratio = 2.0 / sigma_now
    first_scale = sigma_now / HALF_WIDTH
    later_terms = []
    for turn_index in range(2):
        sigma_next = 1.0 / (gamma_ratio - sigma_now)
        later_terms.append((2.0 * sigma_next / HALF_WIDTH, sigma_now * sigma_next))
        sigma_now = sigma_next
    return (first_scale, later_terms)


def up(value, step):
    return (value + step - 1) // step * step


def split3(x):
    high = x.astype(BF16)
    rest = x - high.astype(F32)
    mid = rest.astype(BF16)
    low = (rest - mid.astype(F32)).astype(BF16)
    return high, mid, low


def nn(a, b):
    return lax.dot_general(a, b, (((1,), (0,)), ((), ())), preferred_element_type=F32)


def nt(a, b):
    return lax.dot_general(a, b, (((1,), (1,)), ((), ())), preferred_element_type=F32)


def pick(x, table, dot):
    rows = x.shape[0]
    out = dot(jnp.concatenate(split3(x), axis=0), table)
    return out[:rows] + (out[rows : 2 * rows] + out[2 * rows :])


def full(x, parts, dot):
    rows = x.shape[0]
    high, mid, low = split3(x)
    first = dot(jnp.concatenate([high, mid, low], axis=0), parts[0])
    second = dot(jnp.concatenate([high, mid], axis=0), parts[1])
    third = dot(high, parts[2])
    small = (first[2 * rows :] + second[rows:]) + third
    return first[:rows] + ((first[rows : 2 * rows] + second[:rows]) + small)


def column(row, lanes=128):
    return jnp.broadcast_to(row, (lanes, row.shape[1])).T


def hot(mask):
    return jnp.where(mask, 1.0, 0.0).astype(BF16)


def message(coeffs, atoms):
    return jnp.concatenate([coeffs, jnp.broadcast_to(atoms, (8, atoms.shape[1]))], axis=0)


def enter_kernel(waves, node_map, proj, cells, atoms, x_out, msg_out, parts_out, wide, ids, pad):
    bands, nodes = waves.shape
    ncell, cnodes = node_map.shape
    entries = proj.shape[0]
    width = up(cnodes, 128)
    ids[...] = jnp.full(ids.shape, -1.0, F32)
    for c in range(ncell):
        ids[0:1, c * width : c * width + cnodes] = node_map[c : c + 1, :].astype(F32)
    wide[...] = jnp.zeros(wide.shape, F32)
    wide[:, :nodes] = waves[...]
    place = lax.broadcasted_iota(jnp.int32, (wide.shape[1], ids.shape[1]), 0).astype(F32)
    x = pick(wide[...], hot(place == ids[0:1, :]), nn)
    x_out[...] = x
    pad[...] = jnp.zeros(pad.shape, F32)
    pad[:, :cnodes] = proj[...]
    cell_column = column(cells[...])
    block = pad[...]
    spread = []
    for c in range(ncell):
        for t in range(width // 128):
            keep = cell_column == float(c)
            spread.append(jnp.where(keep, block[:, t * 128 : (t + 1) * 128], 0.0))
    parts = split3(jnp.concatenate(spread, axis=1))
    for k in range(3):
        parts_out[k] = parts[k]
    msg_out[...] = message(full(x, parts, nt), atoms[...])


def table_kernel(node_map, share, parity, matrix, w_out, s_out, m_out, weight_out, ids, face, pad):
    ncell, cnodes = node_map.shape
    faces = share.shape[2]
    width = up(cnodes, 128)
    span = up(faces, 128)
    ids[...] = jnp.full(ids.shape, -1.0, F32)
    for c in range(ncell):
        ids[0:1, c * width : c * width + cnodes] = node_map[c : c + 1, :].astype(F32)
    face[...] = jnp.full(face.shape, -2.0, F32)
    low = share[0, 0:1, :].astype(F32)
    high = share[0, 1:2, :].astype(F32)
    even = parity[...] == 0
    face[0:1, 0:faces] = jnp.where(even, high, low)
    face[0:1, span : span + faces] = jnp.where(even, low, high)
    total = ncell * width
    id_row = ids[0:1, :]
    face_row = face[0:1, :]
    id_column = column(id_row)
    face_column = column(face_row)
    count = jnp.zeros((1, total), F32)
    for t in range(total // 128):
        same = id_column == id_row[:, t * 128 : (t + 1) * 128]
        w_out[:, t * 128 : (t + 1) * 128] = hot(same)
    for t in range(2 * span // 128):
        w_out[:, total + t * 128 : total + (t + 1) * 128] = hot(
            id_column == face_row[:, t * 128 : (t + 1) * 128]
        )
    for t in range(total // 128):
        s_out[:, t * 128 : (t + 1) * 128] = hot(
            face_column == id_row[:, t * 128 : (t + 1) * 128]
        )
    count = nn(jnp.ones((16, total), BF16), w_out[:, :total])
    weight_out[...] = 1.0 / jnp.maximum(count[0:8], 1.0)
    for c in range(ncell):
        pad[...] = jnp.zeros(pad.shape, F32)
        pad[:cnodes, :cnodes] = matrix[c]
        parts = split3(pad[...])
        for k in range(3):
            m_out[k, c] = parts[k]


def cell_kernel(x, m, o_out):
    ncell = m.shape[1]
    width = m.shape[2]
    for c in range(ncell):
        o_out[:, c * width : (c + 1) * width] = full(
            x[:, c * width : (c + 1) * width], [m[k, c] for k in range(3)], nt
        )


def gather_kernel(o, own, m1, m2, m3, m4, atoms, scales, parts, w, v_out, a_out, b_out):
    bands = o.shape[0]
    entries = own.shape[1]
    slots = 8
    atom_column = column(atoms[...])
    row = lax.broadcasted_iota(jnp.int32, (entries, entries), 0)
    col = lax.broadcasted_iota(jnp.int32, (entries, entries), 1)
    same_slot = (row & (slots - 1)) == (col & (slots - 1))
    total = jnp.zeros((bands, entries), F32)
    for near in (own, m1, m2, m3, m4):
        table = hot((atom_column == near[bands : bands + 1, :]) & same_slot)
        total = total + pick(near[:bands, :], table, nt)
    atom_of = lax.broadcasted_iota(jnp.int32, scales.shape, 0).astype(F32)
    scale_row = jnp.sum(
        jnp.where(atom_of == atoms[...], scales[...], 0.0), axis=0, keepdims=True
    )
    returned = total * scale_row
    out = o[...] + full(returned, [parts[k] for k in range(3)], nn)
    spread = pick(out, w[...], nn)
    cells = o.shape[1]
    span = (w.shape[1] - cells) // 2
    v_out[...] = spread[:, :cells]
    a_out[...] = spread[:, cells : cells + span]
    b_out[...] = spread[:, cells + span :]


def step_kernel(lead, back, v, from_a, from_b, s, now, before, parts, atoms, x_out, msg_out):
    incoming = jnp.concatenate([from_a[...], from_b[...]], axis=1)
    operated = v[...] + pick(incoming, s[...], nn)
    x = lead * (operated - CENTER * now[...])
    if back:
        x = x - back * before[...]
    x_out[...] = x
    msg_out[...] = message(full(x, [parts[k] for k in range(3)], nt), atoms[...])


def leave_kernel(
    lead, back, v, from_a, from_b, s, now, before, weight, node_map, share, mass, y_out, z_out, ids
):
    ncell, cnodes = node_map.shape
    bands, nodes = y_out.shape
    width = up(cnodes, 128)
    incoming = jnp.concatenate([from_a[...], from_b[...]], axis=1)
    operated = v[...] + pick(incoming, s[...], nn)
    x = lead * (operated - CENTER * now[...]) - back * before[...]
    ids[...] = jnp.full(ids.shape, -1.0, F32)
    for c in range(ncell):
        ids[0:1, c * width : c * width + cnodes] = node_map[c : c + 1, :].astype(F32)
    whole = up(nodes, 128)
    id_column = column(ids[0:1, :])
    tables = []
    for t in range(whole // 128):
        lane = lax.broadcasted_iota(jnp.int32, (ids.shape[1], 128), 1) + t * 128
        tables.append(hot(id_column == lane.astype(F32)))
    y = pick(x * weight[0:1, :], jnp.concatenate(tables, axis=1), nn)[:, :nodes]
    y_out[...] = y
    low_column = column(share[0, 0:1, :].astype(F32))[:, 0:1]
    lane = lax.broadcasted_iota(jnp.int32, (low_column.shape[0], nodes), 1).astype(F32)
    shared = jnp.max(jnp.where(low_column == lane, 1.0, 0.0), axis=0, keepdims=True)
    z_out[...] = (y * ((1.0 - shared) * jnp.sqrt(mass[...]))).astype(BF16)


def gram_kernel(z, everything, out):
    product = nt(z[...], everything[...])
    across = product.shape[1] // 128
    used = 0
    for r in range(product.shape[0] // 8):
        for c in range(across):
            out[used : used + 8, :] = product[8 * r : 8 * r + 8, 128 * c : 128 * c + 128]
            used += 8
    out[used:, :] = jnp.zeros((out.shape[0] - used, 128), F32)


def sum_kernel(groups, x, out):
    rows = x.shape[0] // groups
    total = x[0:rows, :]
    for k in range(1, groups):
        total = total + x[k * rows : (k + 1) * rows, :]
    for k in range(groups):
        out[k * rows : (k + 1) * rows, :] = total


def finish_kernel(scale, x, first_row, out):
    across = out.shape[1] // 128
    used = 0
    start = first_row[0, 0]
    for r in range(out.shape[0] // 8):
        for c in range(across):
            row = lax.broadcasted_iota(jnp.int32, (8, 128), 0) + (8 * r + start)
            col = lax.broadcasted_iota(jnp.int32, (8, 128), 1) + 128 * c
            out[8 * r : 8 * r + 8, 128 * c : 128 * c + 128] = jnp.where(
                row == col, 0.0, x[used : used + 8, :] / scale
            )
            used += 8


def call(body, outs, scratch=(), smem=()):
    def run(*args):
        specs = [
            pl.BlockSpec(memory_space=pltpu.SMEM if k in smem else pltpu.VMEM)
            for k in range(len(args))
        ]
        return pl.pallas_call(
            body,
            out_shape=[jax.ShapeDtypeStruct(shape, kind) for shape, kind in outs],
            in_specs=specs,
            out_specs=[pl.BlockSpec(memory_space=pltpu.VMEM) for _ in outs],
            scratch_shapes=[pltpu.VMEM(shape, kind) for shape, kind in scratch],
        )(*args)

    return run


def swap(x, stride, inner):
    count = lax.axis_size("cell")
    pairs = []
    for q in range(count):
        ahead = (q // stride) % 2 == (0 if inner else 1)
        pairs.append((q, (q + stride if ahead else q - stride) % count))
    return lax.ppermute(x, "cell", pairs)


def on_device(
    waves, cell_matrix, node_map, share_list, contacts, proj_values, coupling, proj_count, mass
):
    bands, nodes = waves.shape
    ncell, cnodes = node_map.shape
    faces = share_list.shape[2]
    entries, slots = proj_values.shape[:2]
    width = up(cnodes, 128)
    total = ncell * width
    whole = up(nodes, 128)
    span = up(faces, 128)
    flat = entries * slots
    parity = jnp.broadcast_to(lax.axis_index("cell") % 2, (1, 1)).astype(jnp.int32)
    contact_rows = jnp.repeat(contacts, slots, axis=1).astype(F32)
    cells = contact_rows[0:1]
    atoms = contact_rows[1:2]
    levels = jnp.arange(slots, dtype=jnp.int32)
    scales = coupling * (levels[None, :] < proj_count[:, None]).astype(F32)
    scales = jnp.tile(scales, (1, entries))
    proj = proj_values.reshape(flat, cnodes)

    x0, msg, parts = call(
        enter_kernel,
        [((bands, total), F32), ((bands + 8, flat), F32), ((3, flat, total), BF16)],
        [((bands, whole), F32), ((8, total), F32), ((flat, width), F32)],
    )(waves, node_map, proj, cells, atoms)
    w, s, m, weight = call(
        table_kernel,
        [
            ((total, total + 2 * span), BF16),
            ((2 * span, total), BF16),
            ((3, ncell, width, width), BF16),
            ((8, total), F32),
        ],
        [((8, total), F32), ((8, 2 * span), F32), ((width, width), F32)],
    )(node_map, share_list, parity, cell_matrix)

    first_scale, later_terms = filter_terms()
    terms = [(first_scale, 0.0)] + later_terms
    before = x0
    now = x0
    for turn, (lead, back) in enumerate(terms):
        near = [swap(msg, 1, True), swap(msg, 2, True), swap(msg, 1, False), swap(msg, 2, False)]
        (o,) = call(cell_kernel, [((bands, total), F32)])(now, m)
        v, to_a, to_b = call(
            gather_kernel,
            [((bands, total), F32), ((bands, span), F32), ((bands, span), F32)],
        )(o, msg, *near, atoms, scales, parts, w)
        from_a = swap(to_a, 1, True)
        from_b = swap(to_b, 1, False)
        if turn < len(terms) - 1:
            x, msg = call(
                functools.partial(step_kernel, lead, back),
                [((bands, total), F32), ((bands + 8, flat), F32)],
            )(v, from_a, from_b, s, now, before, parts, atoms)
            before, now = now, x
    filtered, zed = call(
        functools.partial(leave_kernel, lead, back),
        [((bands, nodes), F32), ((bands, nodes), BF16)],
        [((8, total), F32)],
    )(v, from_a, from_b, s, now, before, weight, node_map, share_list, mass[None, :])

    groups = lax.axis_size("band")
    count = lax.axis_size("cell")
    everything = lax.all_gather(zed, "band", axis=0, tiled=True)
    tiles = bands // 8 * (bands * groups // 128)
    rows = 8 * up(tiles, count)
    (partial,) = call(gram_kernel, [((rows, 128), F32)])(zed, everything)
    pieces = lax.all_to_all(partial, "cell", 0, 0, tiled=True)
    (summed,) = call(functools.partial(sum_kernel, count), [((rows, 128), F32)])(pieces)
    result = lax.all_to_all(summed, "cell", 0, 0, tiled=True)
    first_row = jnp.broadcast_to(lax.axis_index("band") * bands, (1, 1)).astype(jnp.int32)
    (gram,) = call(
        functools.partial(finish_kernel, math.sqrt(count * nodes)),
        [((bands, bands * groups), F32)],
        smem=(1,),
    )(result, first_row)
    return (filtered, gram)


def solution(mesh):
    return jax.shard_map(
        on_device,
        mesh=mesh,
        in_specs=(
            P("band", "cell"),
            P("cell", None, None),
            P("cell", None),
            P("cell", None, None),
            P(None, "cell"),
            P("cell", None, None),
            P(),
            P(),
            P("cell"),
        ),
        out_specs=(P("band", "cell"), P("band", None)),
        check_vma=False,
    )
```

```python
import functools
import math

import jax
import jax.numpy as jnp
from jax import lax
from jax.experimental import pallas as pl
from jax.experimental.pallas import tpu as pltpu
from jax.sharding import PartitionSpec as P


CENTER = 1.0
HALF_WIDTH = 1.0
LOWEST = -0.5
CORES = 2
CUBE = 8
F32 = jnp.float32
BF16 = jnp.bfloat16


def filter_terms():
    sigma_now = HALF_WIDTH / (LOWEST - CENTER)
    gamma_ratio = 2.0 / sigma_now
    first_scale = sigma_now / HALF_WIDTH
    later_terms = []
    for _ in range(2):
        sigma_next = 1.0 / (gamma_ratio - sigma_now)
        later_terms.append((2.0 * sigma_next / HALF_WIDTH, sigma_now * sigma_next))
        sigma_now = sigma_next
    return (first_scale, later_terms)


def up(value, step):
    return (value + step - 1) // step * step


def split(x, count=2):
    parts = []
    for _ in range(count):
        parts.append(x.astype(BF16))
        x = x - parts[-1].astype(F32)
    return parts


def nn(a, b):
    return lax.dot_general(a, b, (((1,), (0,)), ((), ())), preferred_element_type=F32)


def nt(a, b):
    return lax.dot_general(a, b, (((1,), (1,)), ((), ())), preferred_element_type=F32)


def pick(x, table, dot, count=2):
    rows = x.shape[0]
    out = dot(jnp.concatenate(split(x, count), axis=0), table)
    total = out[(count - 1) * rows :]
    for k in range(count - 2, -1, -1):
        total = out[k * rows : (k + 1) * rows] + total
    return total


def full(x, parts, dot):
    rows = x.shape[0]
    pair = split(x)
    first = dot(jnp.concatenate(pair, axis=0), parts[0])
    return first[:rows] + (first[rows:] + dot(pair[0], parts[1]))


def column(row, lanes=128):
    return jnp.broadcast_to(row, (lanes, row.shape[1])).T


def hot(mask):
    return jnp.where(mask, 1.0, 0.0).astype(BF16)


def message(coeffs, atoms):
    return jnp.concatenate([coeffs, jnp.broadcast_to(atoms, (8, atoms.shape[1]))], axis=0)


def node_row(node_map, ids):
    ncell, cnodes = node_map.shape
    width = ids.shape[1] // ncell
    ids[...] = jnp.full(ids.shape, -1.0, F32)
    for c in range(ncell):
        ids[0:1, c * width : c * width + cnodes] = node_map[c : c + 1, :].astype(F32)
    return ids[0:1, :]


def enter_kernel(waves, node_map, proj, contacts, scales, x_out, msg_out, parts_out, aux_out, wide, ids, pad):
    _, nodes = waves.shape
    ncell, cnodes = node_map.shape
    slots, flat = scales.shape[0], proj.shape[0]
    width = ids.shape[1] // ncell
    id_row = node_row(node_map, ids)
    wide[...] = jnp.zeros(wide.shape, F32)
    wide[:, :nodes] = waves[...]
    place = lax.broadcasted_iota(jnp.int32, (wide.shape[1], ids.shape[1]), 0).astype(F32)
    x = pick(wide[...], hot(place == id_row), nn)
    x_out[...] = x
    entries = contacts.shape[1]
    entry_of = lax.broadcasted_iota(jnp.int32, (entries, flat), 1) // slots
    repeat = hot(entry_of == lax.broadcasted_iota(jnp.int32, (entries, flat), 0))
    both = jnp.concatenate(
        [jnp.broadcast_to(contacts[k : k + 1, :].astype(F32), (8, entries)) for k in range(2)],
        axis=0,
    )
    rows = nn(both.astype(BF16), repeat)
    cells, atoms = rows[0:1], rows[8:9]
    count = scales.shape[1]
    atom_of = lax.broadcasted_iota(jnp.int32, (count, flat), 0).astype(F32)
    by_slot = pick(scales[...], hot(atom_of == atoms), nn, 3)
    slot_of = lax.broadcasted_iota(jnp.int32, (slots, flat), 1) % slots
    mine = slot_of == lax.broadcasted_iota(jnp.int32, (slots, flat), 0)
    scale = jnp.sum(jnp.where(mine, by_slot, 0.0), axis=0, keepdims=True)
    aux_out[0:8, :] = jnp.broadcast_to(atoms, (8, flat))
    aux_out[8:16, :] = jnp.broadcast_to(scale, (8, flat))
    pad[...] = jnp.zeros(pad.shape, F32)
    pad[:, :cnodes] = proj[...]
    cell_column = column(cells)
    block = pad[...]
    spread = []
    for c in range(ncell):
        keep = cell_column == float(c)
        for t in range(width // 128):
            spread.append(jnp.where(keep, block[:, t * 128 : (t + 1) * 128], 0.0))
    parts = split(jnp.concatenate(spread, axis=1))
    for k in range(2):
        parts_out[k] = parts[k]
    msg_out[...] = message(full(x, parts, nt), atoms)


def table_kernel(node_map, share, parity, matrix, w_out, s_out, m_out, weight_out, ids, face, pad, here, sem):
    ncell, cnodes = node_map.shape
    faces = share.shape[2]
    span = face.shape[1] // 2
    copy = pltpu.make_async_copy(matrix, here, sem)
    copy.start()
    id_row = node_row(node_map, ids)
    total = ids.shape[1]
    face[...] = jnp.full(face.shape, -2.0, F32)
    low = share[0, 0:1, :].astype(F32)
    high = share[0, 1:2, :].astype(F32)
    even = parity[...] == 0
    face[0:1, 0:faces] = jnp.where(even, high, low)
    face[0:1, span : span + faces] = jnp.where(even, low, high)
    face_row = face[0:1, :]
    id_column = column(id_row)
    face_column = column(face_row)
    for t in range(total // 128):
        w_out[:, t * 128 : (t + 1) * 128] = hot(id_column == id_row[:, t * 128 : (t + 1) * 128])
    for t in range(2 * span // 128):
        w_out[:, total + t * 128 : total + (t + 1) * 128] = hot(
            id_column == face_row[:, t * 128 : (t + 1) * 128]
        )
    for t in range(total // 128):
        s_out[:, t * 128 : (t + 1) * 128] = hot(
            face_column == id_row[:, t * 128 : (t + 1) * 128]
        )
    count = nn(jnp.ones((16, total), BF16), w_out[:, :total])
    weight_out[...] = 1.0 / jnp.maximum(count[0:8], 1.0)
    pad[...] = jnp.zeros(pad.shape, F32)
    copy.wait()
    for c in range(ncell):
        pad[:cnodes, :cnodes] = here[c]
        parts = split(pad[...])
        for k in range(2):
            m_out[k, c] = parts[k]


def cell_kernel(x, m, o_out):
    ncell = m.shape[1]
    width = m.shape[2]
    for c in range(ncell):
        o_out[:, c * width : (c + 1) * width] = full(
            x[:, c * width : (c + 1) * width], [m[k, c] for k in range(2)], nt
        )


def gather_kernel(o, own, m1, m2, m3, m4, aux, parts, w, v_out, a_out, b_out):
    bands = o.shape[0]
    flat = own.shape[1]
    slots = 8
    atom_column = column(aux[0:1, :])
    row = lax.broadcasted_iota(jnp.int32, (flat, flat), 0)
    col = lax.broadcasted_iota(jnp.int32, (flat, flat), 1)
    same_slot = (row & (slots - 1)) == (col & (slots - 1))
    total = jnp.zeros((bands, flat), F32)
    for near in (own, m1, m2, m3, m4):
        table = hot((atom_column == near[bands : bands + 1, :]) & same_slot)
        total = total + pick(near[:bands, :], table, nt)
    scale_row = aux[8:9, :]
    returned = total * scale_row
    out = o[...] + full(returned, [parts[k] for k in range(2)], nn)
    spread = pick(out, w[...], nn)
    cells = o.shape[1]
    span = (w.shape[1] - cells) // 2
    v_out[...] = spread[:, :cells]
    a_out[...] = spread[:, cells : cells + span]
    b_out[...] = spread[:, cells + span :]


def step_kernel(lead, back, v, from_a, from_b, s, now, before, parts, aux, x_out, msg_out):
    incoming = jnp.concatenate([from_a[...], from_b[...]], axis=1)
    operated = v[...] + pick(incoming, s[...], nn)
    x = lead * (operated - CENTER * now[...])
    if back:
        x = x - back * before[...]
    x_out[...] = x
    msg_out[...] = message(full(x, [parts[k] for k in range(2)], nt), aux[0:1, :])


def leave_kernel(
    lead, back, v, from_a, from_b, s, now, before, weight, node_map, share, mass, y_out, z_out, ids
):
    _, nodes = y_out.shape
    incoming = jnp.concatenate([from_a[...], from_b[...]], axis=1)
    operated = v[...] + pick(incoming, s[...], nn)
    x = lead * (operated - CENTER * now[...]) - back * before[...]
    whole = up(nodes, 128)
    id_column = column(node_row(node_map, ids))
    tables = []
    for t in range(whole // 128):
        lane = lax.broadcasted_iota(jnp.int32, (ids.shape[1], 128), 1) + t * 128
        tables.append(hot(id_column == lane.astype(F32)))
    y = pick(x * weight[0:1, :], jnp.concatenate(tables, axis=1), nn, 3)[:, :nodes]
    y_out[...] = y
    low_column = column(share[0, 0:1, :].astype(F32))[:, 0:1]
    lane = lax.broadcasted_iota(jnp.int32, (low_column.shape[0], nodes), 1).astype(F32)
    shared = jnp.max(jnp.where(low_column == lane, 1.0, 0.0), axis=0, keepdims=True)
    z_out[...] = (y * ((1.0 - shared) * jnp.sqrt(mass[...]))).astype(BF16)


def gram_kernel(bands, left, right, out):
    product = nt(left[...], right[...])
    rows, cols = product.shape
    whole = cols // 128
    used = 0
    for r in range(rows // 8):
        for c in range(whole):
            out[used : used + 8, :] = product[8 * r : 8 * r + 8, 128 * c : 128 * c + 128]
            used += 8
    rest = cols - 128 * whole
    owners = rows // bands
    if rest:
        out[used : used + bands, :] = jnp.concatenate(
            [product[k * bands : (k + 1) * bands, 128 * whole :] for k in range(owners)], axis=1
        )
        used += bands
    if used < out.shape[0]:
        out[used:, :] = jnp.zeros((out.shape[0] - used, 128), F32)


def sum_kernel(groups, x, out):
    rows = x.shape[0] // groups
    total = x[0:rows, :]
    for k in range(1, groups):
        total = total + x[k * rows : (k + 1) * rows, :]
    for k in range(groups):
        out[k * rows : (k + 1) * rows, :] = total


def spread_kernel(bands, scale, x, out):
    rows, cols = out.shape
    whole = cols // 128
    rest = cols - 128 * whole
    used = 0
    for r in range(rows // 8):
        for c in range(whole):
            out[8 * r : 8 * r + 8, 128 * c : 128 * c + 128] = x[used : used + 8, :] / scale
            used += 8
    if rest:
        last = x[used : used + bands, :] / scale
        for k in range(rows // bands):
            out[k * bands : (k + 1) * bands, 128 * whole :] = last[:, k * rest : (k + 1) * rest]


def finish_kernel(first_row, x, out):
    bands, cols = out.shape
    groups = cols // bands
    cubes = groups // CUBE
    blocks = []
    for g in range(groups):
        cube, place, core = g // CUBE, g % CUBE // CORES, g % CORES
        at = (core * cubes + cube) * bands
        blocks.append(x[place * bands : (place + 1) * bands, at : at + bands])
    value = jnp.concatenate(blocks, axis=1)
    row = lax.broadcasted_iota(jnp.int32, value.shape, 0) + first_row[0, 0]
    col = lax.broadcasted_iota(jnp.int32, value.shape, 1)
    out[...] = jnp.where(row == col, 0.0, value)


def call(body, outs, scratch=(), smem=(), hbm=()):
    def run(*args):
        spaces = {**{k: pltpu.SMEM for k in smem}, **{k: pl.ANY for k in hbm}}
        specs = [
            pl.BlockSpec(memory_space=spaces.get(k, pltpu.VMEM)) for k in range(len(args))
        ]
        return pl.pallas_call(
            body,
            out_shape=[jax.ShapeDtypeStruct(shape, kind) for shape, kind in outs],
            in_specs=specs,
            out_specs=[pl.BlockSpec(memory_space=pltpu.VMEM) for _ in outs],
            scratch_shapes=[
                one if not isinstance(one, tuple) else pltpu.VMEM(*one) for one in scratch
            ],
        )(*args)

    return run


def swap(x, stride, inner):
    count = lax.axis_size("cell")
    pairs = []
    for q in range(count):
        ahead = (q // stride) % 2 == (0 if inner else 1)
        pairs.append((q, (q + stride if ahead else q - stride) % count))
    return lax.ppermute(x, "cell", pairs)


def filtered_bands(
    waves, cell_matrix, node_map, share_list, contacts, proj_values, coupling, proj_count, mass
):
    bands, nodes = waves.shape
    ncell, cnodes = node_map.shape
    faces = share_list.shape[2]
    entries, slots = proj_values.shape[:2]
    width = up(cnodes, 128)
    total = ncell * width
    whole = up(nodes, 128)
    span = up(faces, 128)
    flat = entries * slots
    parity = jnp.broadcast_to(lax.axis_index("cell") % 2, (1, 1)).astype(jnp.int32)
    levels = jnp.arange(slots, dtype=jnp.int32)
    scales = jnp.where(levels[None, :] < proj_count[:, None], coupling, 0.0).T
    proj = proj_values.reshape(flat, cnodes)

    x0, msg, parts, aux = call(
        enter_kernel,
        [
            ((bands, total), F32),
            ((bands + 8, flat), F32),
            ((2, flat, total), BF16),
            ((16, flat), F32),
        ],
        [((bands, whole), F32), ((8, total), F32), ((flat, width), F32)],
    )(waves, node_map, proj, contacts, scales)
    w, s, m, weight = call(
        table_kernel,
        [
            ((total, total + 2 * span), BF16),
            ((2 * span, total), BF16),
            ((2, ncell, width, width), BF16),
            ((8, total), F32),
        ],
        [
            ((8, total), F32),
            ((8, 2 * span), F32),
            ((width, width), F32),
            ((ncell, cnodes, cnodes), F32),
            pltpu.SemaphoreType.DMA(()),
        ],
        hbm=(3,),
    )(node_map, share_list, parity, cell_matrix)

    first_scale, later_terms = filter_terms()
    terms = [(first_scale, 0.0)] + later_terms
    before = x0
    now = x0
    for turn, (lead, back) in enumerate(terms):
        near = [swap(msg, 1, True), swap(msg, 2, True), swap(msg, 1, False), swap(msg, 2, False)]
        (o,) = call(cell_kernel, [((bands, total), F32)])(now, m)
        v, to_a, to_b = call(
            gather_kernel,
            [((bands, total), F32), ((bands, span), F32), ((bands, span), F32)],
        )(o, msg, *near, aux, parts, w)
        from_b = swap(to_b, 1, False)
        from_a = swap(to_a, 1, True)
        if turn < len(terms) - 1:
            x, msg = call(
                functools.partial(step_kernel, lead, back),
                [((bands, total), F32), ((bands + 8, flat), F32)],
            )(v, from_a, from_b, s, now, before, parts, aux)
            before, now = now, x
    return call(
        functools.partial(leave_kernel, lead, back),
        [((bands, nodes), F32), ((bands, nodes), BF16)],
        [((8, total), F32)],
    )(v, from_a, from_b, s, now, before, weight, node_map, share_list, mass[None, :])


def inner_products(zed):
    bands, nodes = zed.shape
    groups = lax.axis_size("band")
    count = lax.axis_size("cell")
    cubes, quad = groups // CUBE, CUBE // CORES
    quads = [
        [CUBE * m + CORES * i + k for i in range(quad)] for m in range(cubes) for k in range(CORES)
    ]
    across = [
        [CUBE * m + CORES * i + k for m in range(cubes)] for i in range(quad) for k in range(CORES)
    ]
    chips = [[CORES * i + k for k in range(CORES)] for i in range(groups // CORES)]

    def gather(x, members):
        return lax.all_gather(x, "band", axis=0, tiled=True, axis_index_groups=members)

    left = gather(zed, quads)
    right = gather(gather(zed, across), chips)
    height, wide = left.shape[0], right.shape[0]
    tiles = (height * wide + 1023) // 1024
    rows = 8 * up(tiles, count)
    (partial,) = call(functools.partial(gram_kernel, bands), [((rows, 128), F32)])(left, right)
    pieces = lax.all_to_all(partial, "cell", 0, 0, tiled=True)
    (summed,) = call(functools.partial(sum_kernel, count), [((rows, 128), F32)])(pieces)
    result = lax.all_to_all(summed, "cell", 0, 0, tiled=True)
    (block,) = call(
        functools.partial(spread_kernel, bands, math.sqrt(count * nodes)),
        [((height, wide), F32)],
    )(result)
    mine = lax.all_to_all(block, "band", 0, 0, tiled=True, axis_index_groups=quads)
    first_row = jnp.broadcast_to(lax.axis_index("band") * bands, (1, 1)).astype(jnp.int32)
    (gram,) = call(finish_kernel, [((bands, bands * groups), F32)], smem=(0,))(first_row, mine)
    return gram


def on_device(*args):
    filtered, zed = filtered_bands(*args)
    return (filtered, inner_products(zed))


def solution(mesh):
    return jax.shard_map(
        on_device,
        mesh=mesh,
        in_specs=(
            P("band", "cell"),
            P("cell", None, None),
            P("cell", None),
            P("cell", None, None),
            P(None, "cell"),
            P("cell", None, None),
            P(),
            P(),
            P("cell"),
        ),
        out_specs=(P("band", "cell"), P("band", None)),
        check_vma=False,
    )
```

```python
import functools
import math

import jax
import jax.numpy as jnp
from jax import lax
from jax.experimental import pallas as pl
from jax.experimental.pallas import tpu as pltpu
from jax.sharding import PartitionSpec as P


CENTER = 1.0
HALF_WIDTH = 1.0
LOWEST = -0.5
CORES = 2
CUBE = 8
F32 = jnp.float32
BF16 = jnp.bfloat16


def filter_terms():
    sigma_now = HALF_WIDTH / (LOWEST - CENTER)
    gamma_ratio = 2.0 / sigma_now
    first_scale = sigma_now / HALF_WIDTH
    later_terms = []
    for _ in range(2):
        sigma_next = 1.0 / (gamma_ratio - sigma_now)
        later_terms.append((2.0 * sigma_next / HALF_WIDTH, sigma_now * sigma_next))
        sigma_now = sigma_next
    return (first_scale, later_terms)


def up(value, step):
    return (value + step - 1) // step * step


def split(x, count=2):
    parts = []
    for _ in range(count):
        parts.append(x.astype(BF16))
        x = x - parts[-1].astype(F32)
    return parts


def nn(a, b):
    return lax.dot_general(a, b, (((1,), (0,)), ((), ())), preferred_element_type=F32)


def nt(a, b):
    return lax.dot_general(a, b, (((1,), (1,)), ((), ())), preferred_element_type=F32)


def pick(x, table, dot, count=2):
    rows = x.shape[0]
    out = dot(jnp.concatenate(split(x, count), axis=0), table)
    total = out[(count - 1) * rows :]
    for k in range(count - 2, -1, -1):
        total = out[k * rows : (k + 1) * rows] + total
    return total


def full(x, parts, dot):
    rows = x.shape[0]
    pair = split(x)
    first = dot(jnp.concatenate(pair, axis=0), parts[0])
    return first[:rows] + (first[rows:] + dot(pair[0], parts[1]))


def column(row, lanes=128):
    return jnp.broadcast_to(row, (lanes, row.shape[1])).T


def hot(mask):
    return jnp.where(mask, 1.0, 0.0).astype(BF16)


def message(coeffs, atoms):
    return jnp.concatenate([coeffs, jnp.broadcast_to(atoms, (8, atoms.shape[1]))], axis=0)


def node_row(node_map, ids):
    ncell, cnodes = node_map.shape
    width = ids.shape[1] // ncell
    ids[...] = jnp.full(ids.shape, -1.0, F32)
    for c in range(ncell):
        ids[0:1, c * width : c * width + cnodes] = node_map[c : c + 1, :].astype(F32)
    return ids[0:1, :]


def face_row(share, parity, face):
    faces = share.shape[2]
    span = face.shape[1] // 2
    face[...] = jnp.full(face.shape, -2.0, F32)
    low = share[0, 0:1, :].astype(F32)
    high = share[0, 1:2, :].astype(F32)
    even = parity[...] == 0
    face[0:1, 0:faces] = jnp.where(even, high, low)
    face[0:1, span : span + faces] = jnp.where(even, low, high)
    return face[0:1, :]


def enter_kernel(waves, node_map, proj, contacts, scales, x_out, msg_out, parts_out, aux_out, wide, ids, pad):
    _, nodes = waves.shape
    ncell, cnodes = node_map.shape
    slots, flat = scales.shape[0], proj.shape[0]
    width = ids.shape[1] // ncell
    id_row = node_row(node_map, ids)
    wide[...] = jnp.zeros(wide.shape, F32)
    wide[:, :nodes] = waves[...]
    place = lax.broadcasted_iota(jnp.int32, (wide.shape[1], ids.shape[1]), 0).astype(F32)
    x = pick(wide[...], hot(place == id_row), nn)
    x_out[...] = x
    entries = contacts.shape[1]
    entry_of = lax.broadcasted_iota(jnp.int32, (entries, flat), 1) // slots
    repeat = hot(entry_of == lax.broadcasted_iota(jnp.int32, (entries, flat), 0))
    both = jnp.concatenate(
        [jnp.broadcast_to(contacts[k : k + 1, :].astype(F32), (8, entries)) for k in range(2)],
        axis=0,
    )
    rows = nn(both.astype(BF16), repeat)
    cells, atoms = rows[0:1], rows[8:9]
    count = scales.shape[1]
    atom_of = lax.broadcasted_iota(jnp.int32, (count, flat), 0).astype(F32)
    by_slot = pick(scales[...], hot(atom_of == atoms), nn, 3)
    slot_of = lax.broadcasted_iota(jnp.int32, (slots, flat), 1) % slots
    mine = slot_of == lax.broadcasted_iota(jnp.int32, (slots, flat), 0)
    scale = jnp.sum(jnp.where(mine, by_slot, 0.0), axis=0, keepdims=True)
    aux_out[0:8, :] = jnp.broadcast_to(atoms, (8, flat))
    aux_out[8:16, :] = jnp.broadcast_to(scale, (8, flat))
    pad[...] = jnp.zeros(pad.shape, F32)
    pad[:, :cnodes] = proj[...]
    cell_column = column(cells)
    block = pad[...]
    spread = []
    for c in range(ncell):
        keep = cell_column == float(c)
        for t in range(width // 128):
            spread.append(jnp.where(keep, block[:, t * 128 : (t + 1) * 128], 0.0))
    parts = split(jnp.concatenate(spread, axis=1))
    for k in range(2):
        parts_out[k] = parts[k]
    msg_out[...] = message(full(x, parts, nt), atoms)


def table_kernel(
    node_map, share, parity, matrix, bparts,
    q_out, f_out, s_out, m_out, weight_out, sb_out,
    ids, face, pad, here, sem,
):
    ncell, cnodes = node_map.shape
    span = face.shape[1] // 2
    copy = pltpu.make_async_copy(matrix, here, sem)
    copy.start()
    id_row = node_row(node_map, ids)
    total = ids.shape[1]
    faces_row = face_row(share, parity, face)
    id_column = column(id_row)
    face_column = column(faces_row)
    for t in range(total // 128):
        q_out[:, t * 128 : (t + 1) * 128] = hot(id_column == id_row[:, t * 128 : (t + 1) * 128])
    for t in range(2 * span // 128):
        f_out[:, t * 128 : (t + 1) * 128] = hot(
            id_column == faces_row[:, t * 128 : (t + 1) * 128]
        )
    for t in range(total // 128):
        s_out[:, t * 128 : (t + 1) * 128] = hot(
            face_column == id_row[:, t * 128 : (t + 1) * 128]
        )
    count = nn(jnp.ones((16, total), BF16), q_out[...])
    weight_out[...] = 1.0 / jnp.maximum(count[0:8], 1.0)
    table = s_out[...]
    parts = split(nt(table, bparts[0]) + nt(table, bparts[1]))
    for k in range(2):
        sb_out[k] = parts[k]
    pad[...] = jnp.zeros(pad.shape, F32)
    copy.wait()
    for c in range(ncell):
        pad[:cnodes, :cnodes] = here[c]
        parts = split(pad[...])
        for k in range(2):
            m_out[k, c] = parts[k]


def cell_matrices(x, m, o_out):
    ncell, width = m.shape[1], m.shape[2]
    for c in range(ncell):
        o_out[:, c * width : (c + 1) * width] = full(
            x[:, c * width : (c + 1) * width], [m[k, c] for k in range(2)], nt
        )


def first_kernel(x, m, o_out):
    cell_matrices(x, m, o_out)


def cell_kernel(lead, u, from_a, from_b, s, m, x_out, o_out):
    incoming = jnp.concatenate([from_a[...], from_b[...]], axis=1)
    x_out[...] = u[...] + lead * pick(incoming, s[...], nn)
    cell_matrices(x_out, m, o_out)


def gather_kernel(o, own, m1, m2, m3, m4, aux, parts, f, o_out, a_out, b_out):
    bands = o.shape[0]
    flat = own.shape[1]
    slots = 8
    atom_column = column(aux[0:1, :])
    row = lax.broadcasted_iota(jnp.int32, (flat, flat), 0)
    col = lax.broadcasted_iota(jnp.int32, (flat, flat), 1)
    same_slot = (row & (slots - 1)) == (col & (slots - 1))
    total = jnp.zeros((bands, flat), F32)
    for near in (own, m1, m2, m3, m4):
        table = hot((atom_column == near[bands : bands + 1, :]) & same_slot)
        total = total + pick(near[:bands, :], table, nt)
    scale_row = aux[8:9, :]
    returned = total * scale_row
    out = o[...] + full(returned, [parts[k] for k in range(2)], nn)
    o_out[...] = out
    faces = pick(out, f[...], nn)
    span = a_out.shape[1]
    a_out[...] = faces[:, :span]
    b_out[...] = faces[:, span:]


def inside_kernel(lead, back, o, q, now, before, parts, u_out, c_out):
    u = lead * (pick(o[...], q[...], nn) - CENTER * now[...])
    if back:
        u = u - back * before[...]
    u_out[...] = u
    c_out[...] = full(u, [parts[k] for k in range(2)], nt)


def send_kernel(lead, from_a, from_b, sb, c, aux, msg_out):
    incoming = jnp.concatenate([from_a[...], from_b[...]], axis=1)
    coeffs = c[...] + lead * full(incoming, [sb[k] for k in range(2)], nn)
    msg_out[...] = message(coeffs, aux[0:1, :])


def last_kernel(lead, back, o, now, before, weight, node_map, share, parity, mass, y_out, f_out, z_out, ids, face):
    nodes = mass.shape[1]
    whole = y_out.shape[1]
    span = face.shape[1] // 2
    id_column = column(node_row(node_map, ids))
    face_column = column(face_row(share, parity, face))
    tables = []
    for t in range(whole // 128):
        lane = lax.broadcasted_iota(jnp.int32, (ids.shape[1], 128), 1) + t * 128
        tables.append(hot(id_column == lane.astype(F32)))
        f_out[:, t * 128 : (t + 1) * 128] = hot(
            face_column == lane[: 2 * span].astype(F32)
        )
    past = lead * CENTER * now[...] + back * before[...]
    u = lead * o[...] - past * weight[0:1, :]
    y_out[...] = pick(u, jnp.concatenate(tables, axis=1), nn)
    low_column = column(share[0, 0:1, :].astype(F32))[:, 0:1]
    lane = lax.broadcasted_iota(jnp.int32, (low_column.shape[0], nodes), 1).astype(F32)
    shared = jnp.max(jnp.where(low_column == lane, 1.0, 0.0), axis=0, keepdims=True)
    z_out[...] = jnp.broadcast_to((1.0 - shared) * jnp.sqrt(mass[...]), z_out.shape)


def leave_kernel(lead, y, from_a, from_b, f, z_scale, y_out, z_out, copies_out):
    bands, nodes = y_out.shape
    incoming = jnp.concatenate([from_a[...], from_b[...]], axis=1)
    result = (y[...] + lead * pick(incoming, f[...], nn))[:, :nodes]
    y_out[...] = result
    z = (result * z_scale[0:1, :]).astype(BF16)
    z_out[...] = z
    for k in range(copies_out.shape[0] // bands):
        copies_out[k * bands : (k + 1) * bands, :] = z


def gram_kernel(bands, left, right, out):
    product = nt(left[...], right[...])
    rows, cols = product.shape
    whole = cols // 128
    used = 0
    for r in range(rows // 8):
        for c in range(whole):
            out[used : used + 8, :] = product[8 * r : 8 * r + 8, 128 * c : 128 * c + 128]
            used += 8
    rest = cols - 128 * whole
    owners = rows // bands
    if rest:
        out[used : used + bands, :] = jnp.concatenate(
            [product[k * bands : (k + 1) * bands, 128 * whole :] for k in range(owners)], axis=1
        )
        used += bands
    if used < out.shape[0]:
        out[used:, :] = jnp.zeros((out.shape[0] - used, 128), F32)


def sum_kernel(groups, x, out):
    rows = x.shape[0] // groups
    total = x[0:rows, :]
    for k in range(1, groups):
        total = total + x[k * rows : (k + 1) * rows, :]
    for k in range(groups):
        out[k * rows : (k + 1) * rows, :] = total


def spread_kernel(bands, scale, x, out):
    rows, cols = out.shape
    whole = cols // 128
    rest = cols - 128 * whole
    used = 0
    for r in range(rows // 8):
        for c in range(whole):
            out[8 * r : 8 * r + 8, 128 * c : 128 * c + 128] = x[used : used + 8, :] / scale
            used += 8
    if rest:
        last = x[used : used + bands, :] / scale
        for k in range(rows // bands):
            out[k * bands : (k + 1) * bands, 128 * whole :] = last[:, k * rest : (k + 1) * rest]


def finish_kernel(first_row, x, out):
    bands, cols = out.shape
    groups = cols // bands
    cubes = groups // CUBE
    blocks = []
    for g in range(groups):
        cube, place, core = g // CUBE, g % CUBE // CORES, g % CORES
        at = (core * cubes + cube) * bands
        blocks.append(x[place * bands : (place + 1) * bands, at : at + bands])
    value = jnp.concatenate(blocks, axis=1)
    row = lax.broadcasted_iota(jnp.int32, value.shape, 0) + first_row[0, 0]
    col = lax.broadcasted_iota(jnp.int32, value.shape, 1)
    out[...] = jnp.where(row == col, 0.0, value)


def call(body, outs, scratch=(), smem=(), hbm=()):
    def run(*args):
        spaces = {**{k: pltpu.SMEM for k in smem}, **{k: pl.ANY for k in hbm}}
        specs = [
            pl.BlockSpec(memory_space=spaces.get(k, pltpu.VMEM)) for k in range(len(args))
        ]
        return pl.pallas_call(
            body,
            out_shape=[jax.ShapeDtypeStruct(shape, kind) for shape, kind in outs],
            in_specs=specs,
            out_specs=[pl.BlockSpec(memory_space=pltpu.VMEM) for _ in outs],
            scratch_shapes=[
                one if not isinstance(one, tuple) else pltpu.VMEM(*one) for one in scratch
            ],
        )(*args)

    return run


def swap(x, stride, inner):
    count = lax.axis_size("cell")
    pairs = []
    for q in range(count):
        ahead = (q // stride) % 2 == (0 if inner else 1)
        pairs.append((q, (q + stride if ahead else q - stride) % count))
    return lax.ppermute(x, "cell", pairs)


def filtered_bands(
    waves, cell_matrix, node_map, share_list, contacts, proj_values, coupling, proj_count, mass
):
    bands, nodes = waves.shape
    ncell, cnodes = node_map.shape
    faces = share_list.shape[2]
    entries, slots = proj_values.shape[:2]
    width = up(cnodes, 128)
    total = ncell * width
    whole = up(nodes, 128)
    span = up(faces, 128)
    flat = entries * slots
    parity = jnp.broadcast_to(lax.axis_index("cell") % 2, (1, 1)).astype(jnp.int32)
    levels = jnp.arange(slots, dtype=jnp.int32)
    scales = jnp.where(levels[None, :] < proj_count[:, None], coupling, 0.0).T
    proj = proj_values.reshape(flat, cnodes)

    x0, msg, parts, aux = call(
        enter_kernel,
        [
            ((bands, total), F32),
            ((bands + 8, flat), F32),
            ((2, flat, total), BF16),
            ((16, flat), F32),
        ],
        [((bands, whole), F32), ((8, total), F32), ((flat, width), F32)],
    )(waves, node_map, proj, contacts, scales)
    q, f, s, m, weight, sb = call(
        table_kernel,
        [
            ((total, total), BF16),
            ((total, 2 * span), BF16),
            ((2 * span, total), BF16),
            ((2, ncell, width, width), BF16),
            ((8, total), F32),
            ((2, 2 * span, flat), BF16),
        ],
        [
            ((8, total), F32),
            ((8, 2 * span), F32),
            ((width, width), F32),
            ((ncell, cnodes, cnodes), F32),
            pltpu.SemaphoreType.DMA(()),
        ],
        hbm=(3,),
    )(node_map, share_list, parity, cell_matrix, parts)

    first_scale, later_terms = filter_terms()
    terms = [(first_scale, 0.0)] + later_terms
    block = ((bands, total), F32)
    face_block = ((bands, span), F32)
    before = now = x0
    (o,) = call(first_kernel, [block])(x0, m)
    for turn, (lead, back) in enumerate(terms):
        near = [swap(msg, 1, True), swap(msg, 2, True), swap(msg, 1, False), swap(msg, 2, False)]
        if turn:
            x, o = call(functools.partial(cell_kernel, terms[turn - 1][0]), [block, block])(
                u, from_a, from_b, s, m
            )
            before, now = now, x
        o, to_a, to_b = call(gather_kernel, [block, face_block, face_block])(
            o, msg, *near, aux, parts, f
        )
        from_b = swap(to_b, 1, False)
        from_a = swap(to_a, 1, True)
        if turn < len(terms) - 1:
            u, c = call(
                functools.partial(inside_kernel, lead, back), [block, ((bands, flat), F32)]
            )(o, q, now, before, parts)
            (msg,) = call(functools.partial(send_kernel, lead), [((bands + 8, flat), F32)])(
                from_a, from_b, sb, c, aux
            )
    y, table, z_scale = call(
        functools.partial(last_kernel, lead, back),
        [((bands, whole), F32), ((2 * span, whole), BF16), ((8, nodes), F32)],
        [((8, total), F32), ((8, 2 * span), F32)],
    )(o, now, before, weight, node_map, share_list, parity, mass[None, :])
    copies = lax.axis_size("band") // CUBE
    return call(
        functools.partial(leave_kernel, lead),
        [((bands, nodes), F32), ((bands, nodes), BF16), ((max(copies, 1) * bands, nodes), BF16)],
    )(y, from_a, from_b, table, z_scale)


def inner_products(zed, copies):
    bands, nodes = zed.shape
    groups = lax.axis_size("band")
    count = lax.axis_size("cell")
    cubes, quad = groups // CUBE, CUBE // CORES
    quads = [
        [CUBE * m + CORES * i + k for i in range(quad)] for m in range(cubes) for k in range(CORES)
    ]
    across = [
        [CUBE * m + CORES * i + k for m in range(cubes)] for i in range(quad) for k in range(CORES)
    ]
    chips = [[CORES * i + k for k in range(CORES)] for i in range(groups // CORES)]

    def gather(x, members):
        return lax.all_gather(x, "band", axis=0, tiled=True, axis_index_groups=members)

    left = gather(zed, quads)
    right = lax.all_to_all(copies, "band", 0, 0, tiled=True, axis_index_groups=across)
    right = gather(right, chips)
    height, wide = left.shape[0], right.shape[0]
    tiles = (height * wide + 1023) // 1024
    rows = 8 * up(tiles, count)
    (partial,) = call(functools.partial(gram_kernel, bands), [((rows, 128), F32)])(left, right)
    pieces = lax.all_to_all(partial, "cell", 0, 0, tiled=True)
    (summed,) = call(functools.partial(sum_kernel, count), [((rows, 128), F32)])(pieces)
    result = lax.all_to_all(summed, "cell", 0, 0, tiled=True)
    (block,) = call(
        functools.partial(spread_kernel, bands, math.sqrt(count * nodes)),
        [((height, wide), F32)],
    )(result)
    mine = lax.all_to_all(block, "band", 0, 0, tiled=True, axis_index_groups=quads)
    first_row = jnp.broadcast_to(lax.axis_index("band") * bands, (1, 1)).astype(jnp.int32)
    (gram,) = call(finish_kernel, [((bands, bands * groups), F32)], smem=(0,))(first_row, mine)
    return gram


def on_device(*args):
    filtered, zed, copies = filtered_bands(*args)
    return (filtered, inner_products(zed, copies))


def solution(mesh):
    return jax.shard_map(
        on_device,
        mesh=mesh,
        in_specs=(
            P("band", "cell"),
            P("cell", None, None),
            P("cell", None),
            P("cell", None, None),
            P(None, "cell"),
            P("cell", None, None),
            P(),
            P(),
            P("cell"),
        ),
        out_specs=(P("band", "cell"), P("band", None)),
        check_vma=False,
    )
```

```python
import functools
import math

import jax
import jax.numpy as jnp
from jax import lax
from jax.experimental import pallas as pl
from jax.experimental.pallas import tpu as pltpu
from jax.sharding import PartitionSpec as P


CENTER = 1.0
HALF_WIDTH = 1.0
LOWEST = -0.5
CORES = 2
CUBE = 8
F32 = jnp.float32
BF16 = jnp.bfloat16


def filter_terms():
    sigma_now = HALF_WIDTH / (LOWEST - CENTER)
    gamma_ratio = 2.0 / sigma_now
    first_scale = sigma_now / HALF_WIDTH
    later_terms = []
    for _ in range(2):
        sigma_next = 1.0 / (gamma_ratio - sigma_now)
        later_terms.append((2.0 * sigma_next / HALF_WIDTH, sigma_now * sigma_next))
        sigma_now = sigma_next
    return (first_scale, later_terms)


def up(value, step):
    return (value + step - 1) // step * step


def split(x, count=2):
    parts = []
    for _ in range(count):
        parts.append(x.astype(BF16))
        x = x - parts[-1].astype(F32)
    return parts


def nn(a, b):
    return lax.dot_general(a, b, (((1,), (0,)), ((), ())), preferred_element_type=F32)


def nt(a, b):
    return lax.dot_general(a, b, (((1,), (1,)), ((), ())), preferred_element_type=F32)


def pick(x, table, dot, count=2):
    rows = x.shape[0]
    out = dot(jnp.concatenate(split(x, count), axis=0), table)
    total = out[(count - 1) * rows :]
    for k in range(count - 2, -1, -1):
        total = out[k * rows : (k + 1) * rows] + total
    return total


def full(x, parts, dot):
    rows = x.shape[0]
    pair = split(x)
    first = dot(jnp.concatenate(pair, axis=0), parts[0])
    return first[:rows] + (first[rows:] + dot(pair[0], parts[1]))


def column(row, lanes=128):
    return jnp.broadcast_to(row, (lanes, row.shape[1])).T


def hot(mask):
    return jnp.where(mask, 1.0, 0.0).astype(BF16)


def message(coeffs, atoms):
    return jnp.concatenate([coeffs, jnp.broadcast_to(atoms, (8, atoms.shape[1]))], axis=0)


def node_row(node_map, ids):
    ncell, cnodes = node_map.shape
    width = ids.shape[1] // ncell
    ids[...] = jnp.full(ids.shape, -1.0, F32)
    for c in range(ncell):
        ids[0:1, c * width : c * width + cnodes] = node_map[c : c + 1, :].astype(F32)
    return ids[0:1, :]


def face_row(share, parity, face):
    faces = share.shape[2]
    span = face.shape[1] // 2
    face[...] = jnp.full(face.shape, -2.0, F32)
    low = share[0, 0:1, :].astype(F32)
    high = share[0, 1:2, :].astype(F32)
    even = parity[...] == 0
    face[0:1, 0:faces] = jnp.where(even, high, low)
    face[0:1, span : span + faces] = jnp.where(even, low, high)
    return face[0:1, :]


def enter_kernel(waves, node_map, proj, contacts, scales, x_out, msg_out, parts_out, aux_out, wide, ids, pad):
    _, nodes = waves.shape
    ncell, cnodes = node_map.shape
    slots, flat = scales.shape[0], proj.shape[0]
    width = ids.shape[1] // ncell
    id_row = node_row(node_map, ids)
    wide[...] = jnp.zeros(wide.shape, F32)
    wide[:, :nodes] = waves[...]
    place = lax.broadcasted_iota(jnp.int32, (wide.shape[1], ids.shape[1]), 0).astype(F32)
    x = pick(wide[...], hot(place == id_row), nn)
    x_out[...] = x
    entries = contacts.shape[1]
    entry_of = lax.broadcasted_iota(jnp.int32, (entries, flat), 1) // slots
    repeat = hot(entry_of == lax.broadcasted_iota(jnp.int32, (entries, flat), 0))
    both = jnp.concatenate(
        [jnp.broadcast_to(contacts[k : k + 1, :].astype(F32), (8, entries)) for k in range(2)],
        axis=0,
    )
    rows = nn(both.astype(BF16), repeat)
    cells, atoms = rows[0:1], rows[8:9]
    count = scales.shape[1]
    atom_of = lax.broadcasted_iota(jnp.int32, (count, flat), 0).astype(F32)
    by_slot = pick(scales[...], hot(atom_of == atoms), nn, 3)
    slot_of = lax.broadcasted_iota(jnp.int32, (slots, flat), 1) % slots
    mine = slot_of == lax.broadcasted_iota(jnp.int32, (slots, flat), 0)
    scale = jnp.sum(jnp.where(mine, by_slot, 0.0), axis=0, keepdims=True)
    aux_out[0:8, :] = jnp.broadcast_to(atoms, (8, flat))
    aux_out[8:16, :] = jnp.broadcast_to(scale, (8, flat))
    pad[...] = jnp.zeros(pad.shape, F32)
    pad[:, :cnodes] = proj[...]
    cell_column = column(cells)
    block = pad[...]
    spread = []
    for c in range(ncell):
        keep = cell_column == float(c)
        for t in range(width // 128):
            spread.append(jnp.where(keep, block[:, t * 128 : (t + 1) * 128], 0.0))
    parts = split(jnp.concatenate(spread, axis=1))
    for k in range(2):
        parts_out[k] = parts[k]
    msg_out[...] = message(full(x, parts, nt), atoms)


def table_kernel(
    node_map, share, parity, matrix, bparts,
    q_out, f_out, s_out, m_out, weight_out, sb_out,
    ids, face, pad,
):
    ncell, cnodes = node_map.shape
    span = face.shape[1] // 2
    id_row = node_row(node_map, ids)
    total = ids.shape[1]
    faces_row = face_row(share, parity, face)
    id_column = column(id_row)
    face_column = column(faces_row)
    for t in range(total // 128):
        q_out[:, t * 128 : (t + 1) * 128] = hot(id_column == id_row[:, t * 128 : (t + 1) * 128])
    for t in range(2 * span // 128):
        f_out[:, t * 128 : (t + 1) * 128] = hot(
            id_column == faces_row[:, t * 128 : (t + 1) * 128]
        )
    for t in range(total // 128):
        s_out[:, t * 128 : (t + 1) * 128] = hot(
            face_column == id_row[:, t * 128 : (t + 1) * 128]
        )
    count = nn(jnp.ones((16, total), BF16), q_out[...])
    weight_out[...] = 1.0 / jnp.maximum(count[0:8], 1.0)
    table = s_out[...]
    parts = split(nt(table, bparts[0]) + nt(table, bparts[1]))
    for k in range(2):
        sb_out[k] = parts[k]
    pad[...] = jnp.zeros(pad.shape, F32)
    for c in range(ncell):
        pad[:cnodes, :cnodes] = matrix[c]
        parts = split(pad[...])
        for k in range(2):
            m_out[k, c] = parts[k]


def cell_matrices(x, m, o_out):
    ncell, width = m.shape[1], m.shape[2]
    for c in range(ncell):
        o_out[:, c * width : (c + 1) * width] = full(
            x[:, c * width : (c + 1) * width], [m[k, c] for k in range(2)], nt
        )


def first_kernel(x, m, o_out):
    cell_matrices(x, m, o_out)


def cell_kernel(lead, u, from_a, from_b, s, m, x_out, o_out):
    incoming = jnp.concatenate([from_a[...], from_b[...]], axis=1)
    x_out[...] = u[...] + lead * pick(incoming, s[...], nn)
    cell_matrices(x_out, m, o_out)


def gather_kernel(o, own, m1, m2, m3, m4, aux, parts, f, o_out, a_out, b_out):
    bands = o.shape[0]
    flat = own.shape[1]
    slots = 8
    atom_column = column(aux[0:1, :])
    row = lax.broadcasted_iota(jnp.int32, (flat, flat), 0)
    col = lax.broadcasted_iota(jnp.int32, (flat, flat), 1)
    same_slot = (row & (slots - 1)) == (col & (slots - 1))
    total = jnp.zeros((bands, flat), F32)
    for near in (own, m1, m2, m3, m4):
        table = hot((atom_column == near[bands : bands + 1, :]) & same_slot)
        total = total + pick(near[:bands, :], table, nt)
    scale_row = aux[8:9, :]
    returned = total * scale_row
    out = o[...] + full(returned, [parts[k] for k in range(2)], nn)
    o_out[...] = out
    faces = pick(out, f[...], nn)
    span = a_out.shape[1]
    a_out[...] = faces[:, :span]
    b_out[...] = faces[:, span:]


def inside_kernel(lead, back, o, q, now, before, parts, u_out, c_out):
    u = lead * (pick(o[...], q[...], nn) - CENTER * now[...])
    if back:
        u = u - back * before[...]
    u_out[...] = u
    c_out[...] = full(u, [parts[k] for k in range(2)], nt)


def send_kernel(lead, from_a, from_b, sb, c, aux, msg_out):
    incoming = jnp.concatenate([from_a[...], from_b[...]], axis=1)
    coeffs = c[...] + lead * full(incoming, [sb[k] for k in range(2)], nn)
    msg_out[...] = message(coeffs, aux[0:1, :])


def last_kernel(lead, back, o, now, before, weight, node_map, share, parity, mass, y_out, f_out, z_out, ids, face):
    nodes = mass.shape[1]
    whole = y_out.shape[1]
    span = face.shape[1] // 2
    id_column = column(node_row(node_map, ids))
    face_column = column(face_row(share, parity, face))
    tables = []
    for t in range(whole // 128):
        lane = lax.broadcasted_iota(jnp.int32, (ids.shape[1], 128), 1) + t * 128
        tables.append(hot(id_column == lane.astype(F32)))
        f_out[:, t * 128 : (t + 1) * 128] = hot(
            face_column == lane[: 2 * span].astype(F32)
        )
    past = lead * CENTER * now[...] + back * before[...]
    u = lead * o[...] - past * weight[0:1, :]
    y_out[...] = pick(u, jnp.concatenate(tables, axis=1), nn)
    low_column = column(share[0, 0:1, :].astype(F32))[:, 0:1]
    lane = lax.broadcasted_iota(jnp.int32, (low_column.shape[0], nodes), 1).astype(F32)
    shared = jnp.max(jnp.where(low_column == lane, 1.0, 0.0), axis=0, keepdims=True)
    z_out[...] = jnp.broadcast_to((1.0 - shared) * jnp.sqrt(mass[...]), z_out.shape)


def leave_kernel(lead, y, from_a, from_b, f, z_scale, y_out, z_out, copies_out):
    bands, nodes = y_out.shape
    incoming = jnp.concatenate([from_a[...], from_b[...]], axis=1)
    result = (y[...] + lead * pick(incoming, f[...], nn))[:, :nodes]
    y_out[...] = result
    z = (result * z_scale[0:1, :]).astype(BF16)
    z_out[...] = z
    for k in range(copies_out.shape[0] // bands):
        copies_out[k * bands : (k + 1) * bands, :] = z


def gram_kernel(bands, left, right, out):
    product = nt(left[...], right[...])
    rows, cols = product.shape
    whole = cols // 128
    used = 0
    for r in range(rows // 8):
        for c in range(whole):
            out[used : used + 8, :] = product[8 * r : 8 * r + 8, 128 * c : 128 * c + 128]
            used += 8
    rest = cols - 128 * whole
    owners = rows // bands
    if rest:
        out[used : used + bands, :] = jnp.concatenate(
            [product[k * bands : (k + 1) * bands, 128 * whole :] for k in range(owners)], axis=1
        )
        used += bands
    if used < out.shape[0]:
        out[used:, :] = jnp.zeros((out.shape[0] - used, 128), F32)


def sum_kernel(groups, x, out):
    rows = x.shape[0] // groups
    total = x[0:rows, :]
    for k in range(1, groups):
        total = total + x[k * rows : (k + 1) * rows, :]
    for k in range(groups):
        out[k * rows : (k + 1) * rows, :] = total


def spread_kernel(bands, scale, x, out):
    rows, cols = out.shape
    whole = cols // 128
    rest = cols - 128 * whole
    used = 0
    for r in range(rows // 8):
        for c in range(whole):
            out[8 * r : 8 * r + 8, 128 * c : 128 * c + 128] = x[used : used + 8, :] / scale
            used += 8
    if rest:
        last = x[used : used + bands, :] / scale
        for k in range(rows // bands):
            out[k * bands : (k + 1) * bands, 128 * whole :] = last[:, k * rest : (k + 1) * rest]


def finish_kernel(first_row, x, out):
    bands, cols = out.shape
    groups = cols // bands
    cubes = groups // CUBE
    blocks = []
    for g in range(groups):
        cube, place, core = g // CUBE, g % CUBE // CORES, g % CORES
        at = (core * cubes + cube) * bands
        blocks.append(x[place * bands : (place + 1) * bands, at : at + bands])
    value = jnp.concatenate(blocks, axis=1)
    row = lax.broadcasted_iota(jnp.int32, value.shape, 0) + first_row[0, 0]
    col = lax.broadcasted_iota(jnp.int32, value.shape, 1)
    out[...] = jnp.where(row == col, 0.0, value)


def call(body, outs, scratch=(), smem=(), grant=16):
    def run(*args):
        spaces = {k: pltpu.SMEM for k in smem}
        specs = [
            pl.BlockSpec(memory_space=spaces.get(k, pltpu.VMEM)) for k in range(len(args))
        ]
        return pl.pallas_call(
            body,
            out_shape=[jax.ShapeDtypeStruct(shape, kind) for shape, kind in outs],
            in_specs=specs,
            out_specs=[pl.BlockSpec(memory_space=pltpu.VMEM) for _ in outs],
            scratch_shapes=[
                one if not isinstance(one, tuple) else pltpu.VMEM(*one) for one in scratch
            ],
            compiler_params=pltpu.CompilerParams(vmem_limit_bytes=grant << 20),
        )(*args)

    return run


def swap(x, stride, inner):
    count = lax.axis_size("cell")
    pairs = []
    for q in range(count):
        ahead = (q // stride) % 2 == (0 if inner else 1)
        pairs.append((q, (q + stride if ahead else q - stride) % count))
    return lax.ppermute(x, "cell", pairs)


def filtered_bands(
    waves, cell_matrix, node_map, share_list, contacts, proj_values, coupling, proj_count, mass
):
    bands, nodes = waves.shape
    ncell, cnodes = node_map.shape
    faces = share_list.shape[2]
    entries, slots = proj_values.shape[:2]
    width = up(cnodes, 128)
    total = ncell * width
    whole = up(nodes, 128)
    span = up(faces, 128)
    flat = entries * slots
    parity = jnp.broadcast_to(lax.axis_index("cell") % 2, (1, 1)).astype(jnp.int32)
    levels = jnp.arange(slots, dtype=jnp.int32)
    scales = jnp.where(levels[None, :] < proj_count[:, None], coupling, 0.0).T
    proj = proj_values.reshape(flat, cnodes)

    x0, msg, parts, aux = call(
        enter_kernel,
        [
            ((bands, total), F32),
            ((bands + 8, flat), F32),
            ((2, flat, total), BF16),
            ((16, flat), F32),
        ],
        [((bands, whole), F32), ((8, total), F32), ((flat, width), F32)],
    )(waves, node_map, proj, contacts, scales)
    q, f, s, m, weight, sb = call(
        table_kernel,
        [
            ((total, total), BF16),
            ((total, 2 * span), BF16),
            ((2 * span, total), BF16),
            ((2, ncell, width, width), BF16),
            ((8, total), F32),
            ((2, 2 * span, flat), BF16),
        ],
        [
            ((8, total), F32),
            ((8, 2 * span), F32),
            ((width, width), F32),
        ],
    )(node_map, share_list, parity, cell_matrix, parts)

    first_scale, later_terms = filter_terms()
    terms = [(first_scale, 0.0)] + later_terms
    block = ((bands, total), F32)
    face_block = ((bands, span), F32)
    before = now = x0
    (o,) = call(first_kernel, [block])(x0, m)
    for turn, (lead, back) in enumerate(terms):
        near = [swap(msg, 1, True), swap(msg, 2, True), swap(msg, 1, False), swap(msg, 2, False)]
        if turn:
            x, o = call(functools.partial(cell_kernel, terms[turn - 1][0]), [block, block])(
                u, from_a, from_b, s, m
            )
            before, now = now, x
        o, to_a, to_b = call(gather_kernel, [block, face_block, face_block])(
            o, msg, *near, aux, parts, f
        )
        from_b = swap(to_b, 1, False)
        from_a = swap(to_a, 1, True)
        if turn < len(terms) - 1:
            u, c = call(
                functools.partial(inside_kernel, lead, back), [block, ((bands, flat), F32)]
            )(o, q, now, before, parts)
            (msg,) = call(functools.partial(send_kernel, lead), [((bands + 8, flat), F32)])(
                from_a, from_b, sb, c, aux
            )
    y, table, z_scale = call(
        functools.partial(last_kernel, lead, back),
        [((bands, whole), F32), ((2 * span, whole), BF16), ((8, nodes), F32)],
        [((8, total), F32), ((8, 2 * span), F32)],
    )(o, now, before, weight, node_map, share_list, parity, mass[None, :])
    copies = lax.axis_size("band") // CUBE
    return call(
        functools.partial(leave_kernel, lead),
        [((bands, nodes), F32), ((bands, nodes), BF16), ((max(copies, 1) * bands, nodes), BF16)],
    )(y, from_a, from_b, table, z_scale)


def inner_products(zed, copies):
    bands, nodes = zed.shape
    groups = lax.axis_size("band")
    count = lax.axis_size("cell")
    cubes, quad = groups // CUBE, CUBE // CORES
    quads = [
        [CUBE * m + CORES * i + k for i in range(quad)] for m in range(cubes) for k in range(CORES)
    ]
    across = [
        [CUBE * m + CORES * i + k for m in range(cubes)] for i in range(quad) for k in range(CORES)
    ]
    chips = [[CORES * i + k for k in range(CORES)] for i in range(groups // CORES)]

    def gather(x, members):
        return lax.all_gather(x, "band", axis=0, tiled=True, axis_index_groups=members)

    left = gather(zed, quads)
    right = lax.all_to_all(copies, "band", 0, 0, tiled=True, axis_index_groups=across)
    right = gather(right, chips)
    height, wide = left.shape[0], right.shape[0]
    tiles = (height * wide + 1023) // 1024
    rows = 8 * up(tiles, count)
    (partial,) = call(functools.partial(gram_kernel, bands), [((rows, 128), F32)])(left, right)
    pieces = lax.all_to_all(partial, "cell", 0, 0, tiled=True)
    (summed,) = call(functools.partial(sum_kernel, count), [((rows, 128), F32)])(pieces)
    result = lax.all_to_all(summed, "cell", 0, 0, tiled=True)
    (block,) = call(
        functools.partial(spread_kernel, bands, math.sqrt(count * nodes)),
        [((height, wide), F32)],
    )(result)
    mine = lax.all_to_all(block, "band", 0, 0, tiled=True, axis_index_groups=quads)
    first_row = jnp.broadcast_to(lax.axis_index("band") * bands, (1, 1)).astype(jnp.int32)
    (gram,) = call(finish_kernel, [((bands, bands * groups), F32)], smem=(0,))(first_row, mine)
    return gram


def on_device(*args):
    filtered, zed, copies = filtered_bands(*args)
    return (filtered, inner_products(zed, copies))


def solution(mesh):
    return jax.shard_map(
        on_device,
        mesh=mesh,
        in_specs=(
            P("band", "cell"),
            P("cell", None, None),
            P("cell", None),
            P("cell", None, None),
            P(None, "cell"),
            P("cell", None, None),
            P(),
            P(),
            P("cell"),
        ),
        out_specs=(P("band", "cell"), P("band", None)),
        check_vma=False,
    )
```

```python
import functools
import math

import jax
import jax.numpy as jnp
from jax import lax
from jax.experimental import pallas as pl
from jax.experimental.pallas import tpu as pltpu
from jax.sharding import PartitionSpec as P


CENTER = 1.0
HALF_WIDTH = 1.0
LOWEST = -0.5
CORES = 2
CUBE = 8
SWAPS = ((2, False), (1, False), (2, True), (1, True))
F32 = jnp.float32
BF16 = jnp.bfloat16


def filter_terms():
    sigma_now = HALF_WIDTH / (LOWEST - CENTER)
    gamma_ratio = 2.0 / sigma_now
    first_scale = sigma_now / HALF_WIDTH
    later_terms = []
    for _ in range(2):
        sigma_next = 1.0 / (gamma_ratio - sigma_now)
        later_terms.append((2.0 * sigma_next / HALF_WIDTH, sigma_now * sigma_next))
        sigma_now = sigma_next
    return (first_scale, later_terms)


def up(value, step):
    return (value + step - 1) // step * step


def split(x, count=2):
    parts = []
    for _ in range(count):
        parts.append(x.astype(BF16))
        x = x - parts[-1].astype(F32)
    return parts


def nn(a, b):
    return lax.dot_general(a, b, (((1,), (0,)), ((), ())), preferred_element_type=F32)


def nt(a, b):
    return lax.dot_general(a, b, (((1,), (1,)), ((), ())), preferred_element_type=F32)


def pick(x, table, dot, count=2):
    rows = x.shape[0]
    out = dot(jnp.concatenate(split(x, count), axis=0), table)
    total = out[(count - 1) * rows :]
    for k in range(count - 2, -1, -1):
        total = out[k * rows : (k + 1) * rows] + total
    return total


def full(x, parts, dot):
    rows = x.shape[0]
    pair = split(x)
    first = dot(jnp.concatenate(pair, axis=0), parts[0])
    return first[:rows] + (first[rows:] + dot(pair[0], parts[1]))


def column(row, lanes=128):
    return jnp.broadcast_to(row, (lanes, row.shape[1])).T


def hot(mask):
    return jnp.where(mask, 1.0, 0.0).astype(BF16)


def message(coeffs, atoms):
    return jnp.concatenate([coeffs, jnp.broadcast_to(atoms, (8, atoms.shape[1]))], axis=0)


def node_row(node_map, ids):
    ncell, cnodes = node_map.shape
    width = ids.shape[1] // ncell
    ids[...] = jnp.full(ids.shape, -1.0, F32)
    for c in range(ncell):
        ids[0:1, c * width : c * width + cnodes] = node_map[c : c + 1, :].astype(F32)
    return ids[0:1, :]


def face_row(share, parity, face):
    faces = share.shape[2]
    span = face.shape[1] // 2
    face[...] = jnp.full(face.shape, -2.0, F32)
    low = share[0, 0:1, :].astype(F32)
    high = share[0, 1:2, :].astype(F32)
    even = parity[...] == 0
    face[0:1, 0:faces] = jnp.where(even, high, low)
    face[0:1, span : span + faces] = jnp.where(even, low, high)
    return face[0:1, :]


def enter_kernel(waves, node_map, proj, contacts, scales, x_out, msg_out, parts_out, aux_out, wide, ids, pad):
    _, nodes = waves.shape
    ncell, cnodes = node_map.shape
    slots, flat = scales.shape[0], proj.shape[0]
    width = ids.shape[1] // ncell
    id_row = node_row(node_map, ids)
    wide[...] = jnp.zeros(wide.shape, F32)
    wide[:, :nodes] = waves[...]
    place = lax.broadcasted_iota(jnp.int32, (wide.shape[1], ids.shape[1]), 0).astype(F32)
    x = pick(wide[...], hot(place == id_row), nn)
    x_out[...] = x
    entries = contacts.shape[1]
    entry_of = lax.broadcasted_iota(jnp.int32, (entries, flat), 1) // slots
    repeat = hot(entry_of == lax.broadcasted_iota(jnp.int32, (entries, flat), 0))
    both = jnp.concatenate(
        [jnp.broadcast_to(contacts[k : k + 1, :].astype(F32), (8, entries)) for k in range(2)],
        axis=0,
    )
    rows = nn(both.astype(BF16), repeat)
    cells, atoms = rows[0:1], rows[8:9]
    count = scales.shape[1]
    atom_of = lax.broadcasted_iota(jnp.int32, (count, flat), 0).astype(F32)
    by_slot = pick(scales[...], hot(atom_of == atoms), nn, 3)
    slot_of = lax.broadcasted_iota(jnp.int32, (slots, flat), 1) % slots
    mine = slot_of == lax.broadcasted_iota(jnp.int32, (slots, flat), 0)
    scale = jnp.sum(jnp.where(mine, by_slot, 0.0), axis=0, keepdims=True)
    aux_out[0:8, :] = jnp.broadcast_to(atoms, (8, flat))
    aux_out[8:16, :] = jnp.broadcast_to(scale, (8, flat))
    pad[...] = jnp.zeros(pad.shape, F32)
    pad[:, :cnodes] = proj[...]
    cell_column = column(cells)
    block = pad[...]
    spread = []
    for c in range(ncell):
        keep = cell_column == float(c)
        for t in range(width // 128):
            spread.append(jnp.where(keep, block[:, t * 128 : (t + 1) * 128], 0.0))
    parts = split(jnp.concatenate(spread, axis=1))
    for k in range(2):
        parts_out[k] = parts[k]
    msg_out[...] = message(full(x, parts, nt), atoms)


def table_kernel(
    node_map, share, parity, matrix, bparts,
    q_out, f_out, s_out, m_out, weight_out, sb_out,
    ids, face, pad,
):
    ncell, cnodes = node_map.shape
    span = face.shape[1] // 2
    id_row = node_row(node_map, ids)
    total = ids.shape[1]
    faces_row = face_row(share, parity, face)
    id_column = column(id_row)
    face_column = column(faces_row)
    for t in range(total // 128):
        q_out[:, t * 128 : (t + 1) * 128] = hot(id_column == id_row[:, t * 128 : (t + 1) * 128])
    for t in range(2 * span // 128):
        f_out[:, t * 128 : (t + 1) * 128] = hot(
            id_column == faces_row[:, t * 128 : (t + 1) * 128]
        )
    for t in range(total // 128):
        s_out[:, t * 128 : (t + 1) * 128] = hot(
            face_column == id_row[:, t * 128 : (t + 1) * 128]
        )
    count = nn(jnp.ones((16, total), BF16), q_out[...])
    weight_out[...] = 1.0 / jnp.maximum(count[0:8], 1.0)
    table = s_out[...]
    parts = split(nt(table, bparts[0]) + nt(table, bparts[1]))
    for k in range(2):
        sb_out[k] = parts[k]
    pad[...] = jnp.zeros(pad.shape, F32)
    for c in range(ncell):
        pad[:cnodes, :cnodes] = matrix[c]
        parts = split(pad[...])
        for k in range(2):
            m_out[k, c] = parts[k]


def cell_matrices(x, m, o_out):
    ncell, width = m.shape[1], m.shape[2]
    for c in range(ncell):
        o_out[:, c * width : (c + 1) * width] = full(
            x[:, c * width : (c + 1) * width], [m[k, c] for k in range(2)], nt
        )


def first_kernel(x, m, o_out):
    cell_matrices(x, m, o_out)


def cell_kernel(lead, u, from_a, from_b, s, m, x_out, o_out):
    incoming = jnp.concatenate([from_a[...], from_b[...]], axis=1)
    x_out[...] = u[...] + lead * pick(incoming, s[...], nn)
    cell_matrices(x_out, m, o_out)


def gather_kernel(o, own, m1, m2, m3, m4, aux, parts, f, o_out, a_out, b_out):
    bands = o.shape[0]
    flat = own.shape[1]
    slots = 8
    atom_column = column(aux[0:1, :])
    row = lax.broadcasted_iota(jnp.int32, (flat, flat), 0)
    col = lax.broadcasted_iota(jnp.int32, (flat, flat), 1)
    same_slot = (row & (slots - 1)) == (col & (slots - 1))
    total = jnp.zeros((bands, flat), F32)
    for near in (own, m1, m2, m3, m4):
        table = hot((atom_column == near[bands : bands + 1, :]) & same_slot)
        total = total + pick(near[:bands, :], table, nt)
    scale_row = aux[8:9, :]
    returned = total * scale_row
    out = o[...] + full(returned, [parts[k] for k in range(2)], nn)
    o_out[...] = out
    faces = pick(out, f[...], nn)
    span = a_out.shape[1]
    a_out[...] = faces[:, :span]
    b_out[...] = faces[:, span:]


def inside_kernel(lead, back, o, q, now, before, parts, u_out, c_out):
    u = lead * (pick(o[...], q[...], nn) - CENTER * now[...])
    if back:
        u = u - back * before[...]
    u_out[...] = u
    c_out[...] = full(u, [parts[k] for k in range(2)], nt)


def send_kernel(lead, from_a, from_b, sb, c, aux, msg_out):
    incoming = jnp.concatenate([from_a[...], from_b[...]], axis=1)
    coeffs = c[...] + lead * full(incoming, [sb[k] for k in range(2)], nn)
    msg_out[...] = message(coeffs, aux[0:1, :])


def last_kernel(lead, back, o, now, before, weight, node_map, share, parity, mass, y_out, f_out, z_out, ids, face):
    nodes = mass.shape[1]
    whole = y_out.shape[1]
    span = face.shape[1] // 2
    id_column = column(node_row(node_map, ids))
    face_column = column(face_row(share, parity, face))
    tables = []
    for t in range(whole // 128):
        lane = lax.broadcasted_iota(jnp.int32, (ids.shape[1], 128), 1) + t * 128
        tables.append(hot(id_column == lane.astype(F32)))
        f_out[:, t * 128 : (t + 1) * 128] = hot(
            face_column == lane[: 2 * span].astype(F32)
        )
    past = lead * CENTER * now[...] + back * before[...]
    u = lead * o[...] - past * weight[0:1, :]
    y_out[...] = pick(u, jnp.concatenate(tables, axis=1), nn)
    low_column = column(share[0, 0:1, :].astype(F32))[:, 0:1]
    lane = lax.broadcasted_iota(jnp.int32, (low_column.shape[0], nodes), 1).astype(F32)
    shared = jnp.max(jnp.where(low_column == lane, 1.0, 0.0), axis=0, keepdims=True)
    z_out[...] = jnp.broadcast_to((1.0 - shared) * jnp.sqrt(mass[...]), z_out.shape)


def leave_kernel(lead, y, from_a, from_b, f, z_scale, y_out, z_out, copies_out):
    bands, nodes = y_out.shape
    incoming = jnp.concatenate([from_a[...], from_b[...]], axis=1)
    result = (y[...] + lead * pick(incoming, f[...], nn))[:, :nodes]
    y_out[...] = result
    z = (result * z_scale[0:1, :]).astype(BF16)
    z_out[...] = z
    for k in range(copies_out.shape[0] // bands):
        copies_out[k * bands : (k + 1) * bands, :] = z


def chunk_places(bands, cols):
    whole = cols // 128
    places = [(4 * r, 128 * t) for r in range(bands // 4) for t in range(whole)]
    return whole, places


def gram_kernel(bands, left, right, out):
    product = nt(left[...], right[...])
    rows, cols = product.shape
    owners = rows // bands
    whole, places = chunk_places(bands, cols)
    rest = cols - 128 * whole
    out[...] = jnp.zeros(out.shape, F32)
    height = 4 * owners
    for k in range(owners):
        mine = product[k * bands : (k + 1) * bands]
        chunks = [mine[r : r + 4, t : t + 128] for r, t in places]
        if rest:
            fold = 128 // rest
            tall = bands // fold
            tail = jnp.concatenate(
                [mine[n * tall : (n + 1) * tall, 128 * whole :] for n in range(fold)], axis=1
            )
            chunks += [tail[r : r + 4] for r in range(0, tall, 4)]
        for q, chunk in enumerate(chunks):
            out[q * height + 4 * k : q * height + 4 * k + 4, :] = chunk


def sum_kernel(groups, x, out):
    rows = x.shape[0] // groups
    total = x[0:rows, :]
    for k in range(1, groups):
        total = total + x[k * rows : (k + 1) * rows, :]
    out[...] = total


def finish_kernel(wide, scale, first_row, x, out, blocks):
    bands, cols = out.shape
    groups = cols // bands
    cubes = groups // CUBE
    quad = CUBE // CORES
    height = 4 * quad
    whole, places = chunk_places(bands, wide)
    rest = wide - 128 * whole
    for k in range(quad):
        for q, (r, t) in enumerate(places):
            at = q * height + 4 * k
            blocks[k * bands + r : k * bands + r + 4, t : t + 128] = x[at : at + 4, :]
        if rest:
            fold = 128 // rest
            tall = bands // fold
            for p in range(tall // 4):
                at = (len(places) + p) * height + 4 * k
                for n in range(fold):
                    row = k * bands + n * tall + 4 * p
                    blocks[row : row + 4, 128 * whole : wide] = x[
                        at : at + 4, n * rest : (n + 1) * rest
                    ]
    pieces = []
    for g in range(groups):
        cube, place, core = g // CUBE, g % CUBE // CORES, g % CORES
        at = (core * cubes + cube) * bands
        pieces.append(blocks[place * bands : (place + 1) * bands, at : at + bands])
    value = jnp.concatenate(pieces, axis=1) / scale
    row = lax.broadcasted_iota(jnp.int32, value.shape, 0) + first_row[0, 0]
    col = lax.broadcasted_iota(jnp.int32, value.shape, 1)
    out[...] = jnp.where(row == col, 0.0, value)


def call(body, outs, scratch=(), smem=(), grant=16):
    def run(*args):
        spaces = {k: pltpu.SMEM for k in smem}
        specs = [
            pl.BlockSpec(memory_space=spaces.get(k, pltpu.VMEM)) for k in range(len(args))
        ]
        return pl.pallas_call(
            body,
            out_shape=[jax.ShapeDtypeStruct(shape, kind) for shape, kind in outs],
            in_specs=specs,
            out_specs=[pl.BlockSpec(memory_space=pltpu.VMEM) for _ in outs],
            scratch_shapes=[
                one if not isinstance(one, tuple) else pltpu.VMEM(*one) for one in scratch
            ],
            compiler_params=pltpu.CompilerParams(vmem_limit_bytes=grant << 20),
        )(*args)

    return run


def swap(x, stride, inner):
    count = lax.axis_size("cell")
    pairs = []
    for q in range(count):
        ahead = (q // stride) % 2 == (0 if inner else 1)
        pairs.append((q, (q + stride if ahead else q - stride) % count))
    return lax.ppermute(x, "cell", pairs)


def filtered_bands(
    waves, cell_matrix, node_map, share_list, contacts, proj_values, coupling, proj_count, mass
):
    bands, nodes = waves.shape
    ncell, cnodes = node_map.shape
    faces = share_list.shape[2]
    entries, slots = proj_values.shape[:2]
    width = up(cnodes, 128)
    total = ncell * width
    whole = up(nodes, 128)
    span = up(faces, 128)
    flat = entries * slots
    parity = jnp.broadcast_to(lax.axis_index("cell") % 2, (1, 1)).astype(jnp.int32)
    levels = jnp.arange(slots, dtype=jnp.int32)
    scales = jnp.where(levels[None, :] < proj_count[:, None], coupling, 0.0).T
    proj = proj_values.reshape(flat, cnodes)

    x0, msg, parts, aux = call(
        enter_kernel,
        [
            ((bands, total), F32),
            ((bands + 8, flat), F32),
            ((2, flat, total), BF16),
            ((16, flat), F32),
        ],
        [((bands, whole), F32), ((8, total), F32), ((flat, width), F32)],
    )(waves, node_map, proj, contacts, scales)
    q, f, s, m, weight, sb = call(
        table_kernel,
        [
            ((total, total), BF16),
            ((total, 2 * span), BF16),
            ((2 * span, total), BF16),
            ((2, ncell, width, width), BF16),
            ((8, total), F32),
            ((2, 2 * span, flat), BF16),
        ],
        [
            ((8, total), F32),
            ((8, 2 * span), F32),
            ((width, width), F32),
        ],
    )(node_map, share_list, parity, cell_matrix, parts)

    first_scale, later_terms = filter_terms()
    terms = [(first_scale, 0.0)] + later_terms
    block = ((bands, total), F32)
    face_block = ((bands, span), F32)
    before = now = x0
    (o,) = call(first_kernel, [block])(x0, m)
    for turn, (lead, back) in enumerate(terms):
        near = []
        for stride, inner in SWAPS:
            near.append(swap(msg, stride, inner))
        if turn:
            x, o = call(functools.partial(cell_kernel, terms[turn - 1][0]), [block, block])(
                u, from_a, from_b, s, m
            )
            before, now = now, x
        o, to_a, to_b = call(gather_kernel, [block, face_block, face_block])(
            o, msg, *near, aux, parts, f
        )
        from_b = swap(to_b, 1, False)
        from_a = swap(to_a, 1, True)
        if turn < len(terms) - 1:
            u, c = call(
                functools.partial(inside_kernel, lead, back), [block, ((bands, flat), F32)]
            )(o, q, now, before, parts)
            (msg,) = call(functools.partial(send_kernel, lead), [((bands + 8, flat), F32)])(
                from_a, from_b, sb, c, aux
            )
    y, table, z_scale = call(
        functools.partial(last_kernel, lead, back),
        [((bands, whole), F32), ((2 * span, whole), BF16), ((8, nodes), F32)],
        [((8, total), F32), ((8, 2 * span), F32)],
    )(o, now, before, weight, node_map, share_list, parity, mass[None, :])
    copies = lax.axis_size("band") // CUBE
    return call(
        functools.partial(leave_kernel, lead),
        [((bands, nodes), F32), ((bands, nodes), BF16), ((max(copies, 1) * bands, nodes), BF16)],
    )(y, from_a, from_b, table, z_scale)


def inner_products(zed, copies):
    bands, nodes = zed.shape
    groups = lax.axis_size("band")
    count = lax.axis_size("cell")
    cubes, quad = groups // CUBE, CUBE // CORES
    quads = [
        [CUBE * m + CORES * i + k for i in range(quad)] for m in range(cubes) for k in range(CORES)
    ]
    across = [
        [CUBE * m + CORES * i + k for m in range(cubes)] for i in range(quad) for k in range(CORES)
    ]
    chips = [[CORES * i + k for k in range(CORES)] for i in range(groups // CORES)]

    def gather(x, members):
        return lax.all_gather(x, "band", axis=0, tiled=True, axis_index_groups=members)

    left = gather(zed, quads)
    right = lax.all_to_all(copies, "band", 0, 0, tiled=True, axis_index_groups=across)
    right = gather(right, chips)
    height, wide = left.shape[0], right.shape[0]
    rows = 4 * quad
    (partial,) = call(functools.partial(gram_kernel, bands), [((count * rows, 128), F32)])(
        left, right
    )
    pieces = lax.all_to_all(partial, "cell", 0, 0, tiled=True)
    (summed,) = call(functools.partial(sum_kernel, count), [((rows, 128), F32)])(pieces)
    mine = lax.all_to_all(summed, "band", 0, 0, tiled=True, axis_index_groups=quads)
    result = lax.all_to_all(jnp.tile(mine, (count, 1)), "cell", 0, 0, tiled=True)
    first_row = jnp.broadcast_to(lax.axis_index("band") * bands, (1, 1)).astype(jnp.int32)
    (gram,) = call(
        functools.partial(finish_kernel, wide, math.sqrt(count * nodes)),
        [((bands, bands * groups), F32)],
        [((height, up(wide, 128)), F32)],
        smem=(0,),
    )(first_row, result)
    return gram


def on_device(*args):
    filtered, zed, copies = filtered_bands(*args)
    return (filtered, inner_products(zed, copies))


def solution(mesh):
    return jax.shard_map(
        on_device,
        mesh=mesh,
        in_specs=(
            P("band", "cell"),
            P("cell", None, None),
            P("cell", None),
            P("cell", None, None),
            P(None, "cell"),
            P("cell", None, None),
            P(),
            P(),
            P("cell"),
        ),
        out_specs=(P("band", "cell"), P("band", None)),
        check_vma=False,
    )
```

```python
import functools
import math

import jax
import jax.numpy as jnp
from jax import lax
from jax.experimental import pallas as pl
from jax.experimental.pallas import tpu as pltpu
from jax.sharding import PartitionSpec as P


CENTER = 1.0
HALF_WIDTH = 1.0
LOWEST = -0.5
CORES = 2
CUBE = 8
SWAPS = ((2, False), (1, False), (2, True), (1, True))
F32 = jnp.float32
BF16 = jnp.bfloat16


def filter_terms():
    sigma_now = HALF_WIDTH / (LOWEST - CENTER)
    gamma_ratio = 2.0 / sigma_now
    first_scale = sigma_now / HALF_WIDTH
    later_terms = []
    for _ in range(2):
        sigma_next = 1.0 / (gamma_ratio - sigma_now)
        later_terms.append((2.0 * sigma_next / HALF_WIDTH, sigma_now * sigma_next))
        sigma_now = sigma_next
    return (first_scale, later_terms)


def up(value, step):
    return (value + step - 1) // step * step


def split(x, count=2):
    parts = []
    for _ in range(count):
        parts.append(x.astype(BF16))
        x = x - parts[-1].astype(F32)
    return parts


def nn(a, b):
    return lax.dot_general(a, b, (((1,), (0,)), ((), ())), preferred_element_type=F32)


def nt(a, b):
    return lax.dot_general(a, b, (((1,), (1,)), ((), ())), preferred_element_type=F32)


def pick(x, table, dot, count=2):
    rows = x.shape[0]
    out = dot(jnp.concatenate(split(x, count), axis=0), table)
    total = out[(count - 1) * rows :]
    for k in range(count - 2, -1, -1):
        total = out[k * rows : (k + 1) * rows] + total
    return total


def full(x, parts, dot):
    rows = x.shape[0]
    pair = split(x)
    first = dot(jnp.concatenate(pair, axis=0), parts[0])
    return first[:rows] + (first[rows:] + dot(pair[0], parts[1]))


def column(row, lanes=128):
    return jnp.broadcast_to(row, (lanes, row.shape[1])).T


def hot(mask):
    return jnp.where(mask, 1.0, 0.0).astype(BF16)


def message(coeffs, atoms):
    return jnp.concatenate([coeffs, jnp.broadcast_to(atoms, (8, atoms.shape[1]))], axis=0)


def node_row(node_map, ids):
    ncell, cnodes = node_map.shape
    width = ids.shape[1] // ncell
    ids[...] = jnp.full(ids.shape, -1.0, F32)
    for c in range(ncell):
        ids[0:1, c * width : c * width + cnodes] = node_map[c : c + 1, :].astype(F32)
    return ids[0:1, :]


def face_row(share, parity, face):
    faces = share.shape[2]
    span = face.shape[1] // 2
    face[...] = jnp.full(face.shape, -2.0, F32)
    low = share[0, 0:1, :].astype(F32)
    high = share[0, 1:2, :].astype(F32)
    even = parity[...] == 0
    face[0:1, 0:faces] = jnp.where(even, high, low)
    face[0:1, span : span + faces] = jnp.where(even, low, high)
    return face[0:1, :]


def enter_kernel(
    waves, node_map, proj, contacts, scales, x_out, msg_out, parts_out, aux_out, wide, ids, pad
):
    _, nodes = waves.shape
    ncell, cnodes = node_map.shape
    slots, flat = scales.shape[0], proj.shape[0]
    width = ids.shape[1] // ncell
    id_row = node_row(node_map, ids)
    wide[...] = jnp.zeros(wide.shape, F32)
    wide[:, :nodes] = waves[...]
    place = lax.broadcasted_iota(jnp.int32, (wide.shape[1], ids.shape[1]), 0).astype(F32)
    x = pick(wide[...], hot(place == id_row), nn)
    x_out[...] = x
    entries = contacts.shape[1]
    entry_of = lax.broadcasted_iota(jnp.int32, (entries, flat), 1) // slots
    repeat = hot(entry_of == lax.broadcasted_iota(jnp.int32, (entries, flat), 0))
    both = jnp.concatenate(
        [jnp.broadcast_to(contacts[k : k + 1, :].astype(F32), (8, entries)) for k in range(2)],
        axis=0,
    )
    rows = nn(both.astype(BF16), repeat)
    cells, atoms = rows[0:1], rows[8:9]
    count = scales.shape[1]
    atom_of = lax.broadcasted_iota(jnp.int32, (count, flat), 0).astype(F32)
    by_slot = pick(scales[...], hot(atom_of == atoms), nn, 3)
    slot_of = lax.broadcasted_iota(jnp.int32, (slots, flat), 1) % slots
    mine = slot_of == lax.broadcasted_iota(jnp.int32, (slots, flat), 0)
    scale = jnp.sum(jnp.where(mine, by_slot, 0.0), axis=0, keepdims=True)
    aux_out[0:8, :] = jnp.broadcast_to(atoms, (8, flat))
    aux_out[8:16, :] = jnp.broadcast_to(scale, (8, flat))
    pad[...] = jnp.zeros(pad.shape, F32)
    pad[:, :cnodes] = proj[...]
    cell_column = column(cells)
    block = pad[...]
    spread = []
    for c in range(ncell):
        keep = cell_column == float(c)
        for t in range(width // 128):
            spread.append(jnp.where(keep, block[:, t * 128 : (t + 1) * 128], 0.0))
    parts = split(jnp.concatenate(spread, axis=1))
    for k in range(2):
        parts_out[k] = parts[k]
    msg_out[...] = message(full(x, parts, nt), atoms)


def table_kernel(node_map, share, parity, matrix, f_out, m_out, ids, face, pad):
    ncell, cnodes = node_map.shape
    id_column = column(node_row(node_map, ids))
    faces_row = face_row(share, parity, face)
    for t in range(face.shape[1] // 128):
        f_out[:, t * 128 : (t + 1) * 128] = hot(
            id_column == faces_row[:, t * 128 : (t + 1) * 128]
        )
    pad[...] = jnp.zeros(pad.shape, F32)
    for c in range(ncell):
        pad[:cnodes, :cnodes] = matrix[c]
        parts = split(pad[...])
        for k in range(2):
            m_out[k, c] = parts[k]


def inside_first_kernel(
    lead, o, now, bparts, node_map, share, parity,
    u_out, c_out, q_out, s_out, sb_out, weight_out,
    ids, face,
):
    id_row = node_row(node_map, ids)
    total = ids.shape[1]
    id_column = column(id_row)
    face_column = column(face_row(share, parity, face))
    for t in range(total // 128):
        q_out[:, t * 128 : (t + 1) * 128] = hot(id_column == id_row[:, t * 128 : (t + 1) * 128])
        s_out[:, t * 128 : (t + 1) * 128] = hot(
            face_column == id_row[:, t * 128 : (t + 1) * 128]
        )
    inside_kernel(lead, 0.0, o, q_out, now, now, bparts, u_out, c_out)
    table = s_out[...]
    parts = split(nt(table, bparts[0]) + nt(table, bparts[1]))
    for k in range(2):
        sb_out[k] = parts[k]
    count = nn(jnp.ones((16, total), BF16), q_out[...])
    weight_out[...] = 1.0 / jnp.maximum(count[0:8], 1.0)


def cell_matrices(x, m, o_out):
    ncell, width = m.shape[1], m.shape[2]
    for c in range(ncell):
        o_out[:, c * width : (c + 1) * width] = full(
            x[:, c * width : (c + 1) * width], [m[k, c] for k in range(2)], nt
        )


def first_kernel(x, m, o_out):
    cell_matrices(x, m, o_out)


def cell_kernel(lead, u, from_a, from_b, s, m, x_out, o_out):
    incoming = jnp.concatenate([from_a[...], from_b[...]], axis=1)
    x_out[...] = u[...] + lead * pick(incoming, s[...], nn)
    cell_matrices(x_out, m, o_out)


def gather_kernel(o, own, m1, m2, m3, m4, aux, parts, f, o_out, a_out, b_out):
    bands = o.shape[0]
    flat = own.shape[1]
    slots = 8
    atom_column = column(aux[0:1, :])
    row = lax.broadcasted_iota(jnp.int32, (flat, flat), 0)
    col = lax.broadcasted_iota(jnp.int32, (flat, flat), 1)
    same_slot = (row & (slots - 1)) == (col & (slots - 1))
    total = jnp.zeros((bands, flat), F32)
    for near in (own, m1, m2, m3, m4):
        table = hot((atom_column == near[bands : bands + 1, :]) & same_slot)
        total = total + pick(near[:bands, :], table, nt)
    scale_row = aux[8:9, :]
    returned = total * scale_row
    out = o[...] + full(returned, [parts[k] for k in range(2)], nn)
    o_out[...] = out
    faces = pick(out, f[...], nn)
    span = a_out.shape[1]
    a_out[...] = faces[:, :span]
    b_out[...] = faces[:, span:]


def inside_kernel(lead, back, o, q, now, before, parts, u_out, c_out):
    u = lead * (pick(o[...], q[...], nn) - CENTER * now[...])
    if back:
        u = u - back * before[...]
    u_out[...] = u
    c_out[...] = full(u, [parts[k] for k in range(2)], nt)


def send_kernel(lead, from_a, from_b, sb, c, aux, msg_out):
    incoming = jnp.concatenate([from_a[...], from_b[...]], axis=1)
    coeffs = c[...] + lead * full(incoming, [sb[k] for k in range(2)], nn)
    msg_out[...] = message(coeffs, aux[0:1, :])


def last_kernel(lead, back, o, now, before, weight, node_map, share, parity, mass, y_out, f_out, z_out, ids, face):
    nodes = mass.shape[1]
    whole = y_out.shape[1]
    span = face.shape[1] // 2
    id_column = column(node_row(node_map, ids))
    face_column = column(face_row(share, parity, face))
    tables = []
    for t in range(whole // 128):
        lane = lax.broadcasted_iota(jnp.int32, (ids.shape[1], 128), 1) + t * 128
        tables.append(hot(id_column == lane.astype(F32)))
        f_out[:, t * 128 : (t + 1) * 128] = hot(
            face_column == lane[: 2 * span].astype(F32)
        )
    past = lead * CENTER * now[...] + back * before[...]
    u = lead * o[...] - past * weight[0:1, :]
    y_out[...] = pick(u, jnp.concatenate(tables, axis=1), nn)
    low_column = column(share[0, 0:1, :].astype(F32))[:, 0:1]
    lane = lax.broadcasted_iota(jnp.int32, (low_column.shape[0], nodes), 1).astype(F32)
    shared = jnp.max(jnp.where(low_column == lane, 1.0, 0.0), axis=0, keepdims=True)
    z_out[...] = jnp.broadcast_to((1.0 - shared) * jnp.sqrt(mass[...]), z_out.shape)


def leave_kernel(lead, y, from_a, from_b, f, z_scale, y_out, z_out, copies_out):
    bands, nodes = y_out.shape
    incoming = jnp.concatenate([from_a[...], from_b[...]], axis=1)
    result = (y[...] + lead * pick(incoming, f[...], nn))[:, :nodes]
    y_out[...] = result
    z = (result * z_scale[0:1, :]).astype(BF16)
    z_out[...] = z
    for k in range(copies_out.shape[0] // bands):
        copies_out[k * bands : (k + 1) * bands, :] = z


def chunk_places(bands, cols):
    whole = cols // 128
    places = [(4 * r, 128 * t) for r in range(bands // 4) for t in range(whole)]
    return whole, places


def gram_kernel(bands, left, right, out):
    product = nt(left[...], right[...])
    rows, cols = product.shape
    owners = rows // bands
    whole, places = chunk_places(bands, cols)
    rest = cols - 128 * whole
    out[...] = jnp.zeros(out.shape, F32)
    height = 4 * owners
    for k in range(owners):
        mine = product[k * bands : (k + 1) * bands]
        chunks = [mine[r : r + 4, t : t + 128] for r, t in places]
        if rest:
            fold = 128 // rest
            tall = bands // fold
            tail = jnp.concatenate(
                [mine[n * tall : (n + 1) * tall, 128 * whole :] for n in range(fold)], axis=1
            )
            chunks += [tail[r : r + 4] for r in range(0, tall, 4)]
        for q, chunk in enumerate(chunks):
            out[q * height + 4 * k : q * height + 4 * k + 4, :] = chunk


def sum_kernel(groups, x, out):
    rows = x.shape[0] // groups
    total = x[0:rows, :]
    for k in range(1, groups):
        total = total + x[k * rows : (k + 1) * rows, :]
    out[...] = total


def finish_kernel(wide, scale, first_row, x, out, blocks):
    bands, cols = out.shape
    groups = cols // bands
    cubes = groups // CUBE
    quad = CUBE // CORES
    height = 4 * quad
    whole, places = chunk_places(bands, wide)
    rest = wide - 128 * whole
    for k in range(quad):
        for q, (r, t) in enumerate(places):
            at = q * height + 4 * k
            blocks[k * bands + r : k * bands + r + 4, t : t + 128] = x[at : at + 4, :]
        if rest:
            fold = 128 // rest
            tall = bands // fold
            for p in range(tall // 4):
                at = (len(places) + p) * height + 4 * k
                for n in range(fold):
                    row = k * bands + n * tall + 4 * p
                    blocks[row : row + 4, 128 * whole : wide] = x[
                        at : at + 4, n * rest : (n + 1) * rest
                    ]
    pieces = []
    for g in range(groups):
        cube, place, core = g // CUBE, g % CUBE // CORES, g % CORES
        at = (core * cubes + cube) * bands
        pieces.append(blocks[place * bands : (place + 1) * bands, at : at + bands])
    value = jnp.concatenate(pieces, axis=1) / scale
    row = lax.broadcasted_iota(jnp.int32, value.shape, 0) + first_row[0, 0]
    col = lax.broadcasted_iota(jnp.int32, value.shape, 1)
    out[...] = jnp.where(row == col, 0.0, value)


def call(body, outs, scratch=(), smem=(), grant=16):
    def run(*args):
        spaces = {k: pltpu.SMEM for k in smem}
        specs = [
            pl.BlockSpec(memory_space=spaces.get(k, pltpu.VMEM)) for k in range(len(args))
        ]
        return pl.pallas_call(
            body,
            out_shape=[jax.ShapeDtypeStruct(shape, kind) for shape, kind in outs],
            in_specs=specs,
            out_specs=[pl.BlockSpec(memory_space=pltpu.VMEM) for _ in outs],
            scratch_shapes=[pltpu.VMEM(shape, kind) for shape, kind in scratch],
            compiler_params=pltpu.CompilerParams(vmem_limit_bytes=grant << 20),
        )(*args)

    return run


def swap(x, stride, inner):
    count = lax.axis_size("cell")
    pairs = []
    for q in range(count):
        ahead = (q // stride) % 2 == (0 if inner else 1)
        pairs.append((q, (q + stride if ahead else q - stride) % count))
    return lax.ppermute(x, "cell", pairs)


def filtered_bands(
    waves, cell_matrix, node_map, share_list, contacts, proj_values, coupling, proj_count, mass
):
    bands, nodes = waves.shape
    ncell, cnodes = node_map.shape
    faces = share_list.shape[2]
    entries, slots = proj_values.shape[:2]
    width = up(cnodes, 128)
    total = ncell * width
    whole = up(nodes, 128)
    span = up(faces, 128)
    flat = entries * slots
    parity = jnp.broadcast_to(lax.axis_index("cell") % 2, (1, 1)).astype(jnp.int32)
    levels = jnp.arange(slots, dtype=jnp.int32)
    scales = jnp.where(levels[None, :] < proj_count[:, None], coupling, 0.0).T
    proj = proj_values.reshape(flat, cnodes)

    x0, msg, parts, aux = call(
        enter_kernel,
        [
            ((bands, total), F32),
            ((bands + 8, flat), F32),
            ((2, flat, total), BF16),
            ((16, flat), F32),
        ],
        [((bands, whole), F32), ((8, total), F32), ((flat, width), F32)],
    )(waves, node_map, proj, contacts, scales)
    f, m = call(
        table_kernel,
        [((total, 2 * span), BF16), ((2, ncell, width, width), BF16)],
        [((8, total), F32), ((8, 2 * span), F32), ((width, width), F32)],
    )(node_map, share_list, parity, cell_matrix)

    first_scale, later_terms = filter_terms()
    terms = [(first_scale, 0.0)] + later_terms
    block = ((bands, total), F32)
    face_block = ((bands, span), F32)
    before = now = x0
    (o,) = call(first_kernel, [block])(x0, m)
    for turn, (lead, back) in enumerate(terms):
        near = []
        for stride, inner in SWAPS:
            near.append(swap(msg, stride, inner))
        if turn:
            x, o = call(functools.partial(cell_kernel, terms[turn - 1][0]), [block, block])(
                u, from_a, from_b, s, m
            )
            before, now = now, x
        o, to_a, to_b = call(gather_kernel, [block, face_block, face_block])(
            o, msg, *near, aux, parts, f
        )
        from_b = swap(to_b, 1, False)
        from_a = swap(to_a, 1, True)
        if turn == 0:
            u, c, q, s, sb, weight = call(
                functools.partial(inside_first_kernel, lead),
                [
                    block,
                    ((bands, flat), F32),
                    ((total, total), BF16),
                    ((2 * span, total), BF16),
                    ((2, 2 * span, flat), BF16),
                    ((8, total), F32),
                ],
                [((8, total), F32), ((8, 2 * span), F32)],
            )(o, now, parts, node_map, share_list, parity)
        elif turn < len(terms) - 1:
            u, c = call(
                functools.partial(inside_kernel, lead, back), [block, ((bands, flat), F32)]
            )(o, q, now, before, parts)
        if turn < len(terms) - 1:
            (msg,) = call(functools.partial(send_kernel, lead), [((bands + 8, flat), F32)])(
                from_a, from_b, sb, c, aux
            )
    y, table, z_scale = call(
        functools.partial(last_kernel, lead, back),
        [((bands, whole), F32), ((2 * span, whole), BF16), ((8, nodes), F32)],
        [((8, total), F32), ((8, 2 * span), F32)],
    )(o, now, before, weight, node_map, share_list, parity, mass[None, :])
    copies = lax.axis_size("band") // CUBE
    return call(
        functools.partial(leave_kernel, lead),
        [((bands, nodes), F32), ((bands, nodes), BF16), ((max(copies, 1) * bands, nodes), BF16)],
    )(y, from_a, from_b, table, z_scale)


def inner_products(zed, copies):
    bands, nodes = zed.shape
    groups = lax.axis_size("band")
    count = lax.axis_size("cell")
    cubes, quad = groups // CUBE, CUBE // CORES
    quads = [
        [CUBE * m + CORES * i + k for i in range(quad)] for m in range(cubes) for k in range(CORES)
    ]
    across = [
        [CUBE * m + CORES * i + k for m in range(cubes)] for i in range(quad) for k in range(CORES)
    ]
    chips = [[CORES * i + k for k in range(CORES)] for i in range(groups // CORES)]

    def gather(x, members):
        return lax.all_gather(x, "band", axis=0, tiled=True, axis_index_groups=members)

    left = gather(zed, quads)
    right = lax.all_to_all(copies, "band", 0, 0, tiled=True, axis_index_groups=across)
    right = gather(right, chips)
    height, wide = left.shape[0], right.shape[0]
    rows = 4 * quad
    (partial,) = call(functools.partial(gram_kernel, bands), [((count * rows, 128), F32)])(
        left, right
    )
    pieces = lax.all_to_all(partial, "cell", 0, 0, tiled=True)
    (summed,) = call(functools.partial(sum_kernel, count), [((rows, 128), F32)])(pieces)
    mine = lax.all_to_all(summed, "band", 0, 0, tiled=True, axis_index_groups=quads)
    result = lax.all_to_all(jnp.tile(mine, (count, 1)), "cell", 0, 0, tiled=True)
    first_row = jnp.broadcast_to(lax.axis_index("band") * bands, (1, 1)).astype(jnp.int32)
    (gram,) = call(
        functools.partial(finish_kernel, wide, math.sqrt(count * nodes)),
        [((bands, bands * groups), F32)],
        [((height, up(wide, 128)), F32)],
        smem=(0,),
    )(first_row, result)
    return gram


def on_device(*args):
    filtered, zed, copies = filtered_bands(*args)
    return (filtered, inner_products(zed, copies))


def solution(mesh):
    return jax.shard_map(
        on_device,
        mesh=mesh,
        in_specs=(
            P("band", "cell"),
            P("cell", None, None),
            P("cell", None),
            P("cell", None, None),
            P(None, "cell"),
            P("cell", None, None),
            P(),
            P(),
            P("cell"),
        ),
        out_specs=(P("band", "cell"), P("band", None)),
        check_vma=False,
    )
```
